32 devices in a mesh: inl: 4 (over x, core), xl: 8 (over z, y).
Axes of the slice: x: 2, y: 2, z: 4, core: 2. Of those that a mesh axis runs over, the one named last changes fastest.
Arguments:
- baseline: float32 [16, 128, 1024], P('inl', 'xl'), may hold values from -600 to 600
- monitor: float32 [16, 128, 1024], P('inl', 'xl'), may hold values from -900 to 900
- shift_model: float32 [4, 32, 128], P(None, None, 'xl'), may hold values from -4 to 4
- knot_start: int32 [32, 4], replicated, may hold values from -12 to 13, as said below
- half_width: int32 [8], P('xl'), may hold values from 1 to 3
Outputs:
- shift_obs: float32 [16, 128, 1024], P('inl', 'xl')
- delta: float32 [4, 32, 128], P(None, 'xl', 'inl')
The draws below stay inside these ranges and needn't reach their ends.
Inputs may be any that keep to these rules, and one draw needn't show every extreme that they name: `knot_start`: basis function k of a window starts at sample k * 8 - 3 * 4 or one later, relative to the window's first sample.
All inputs are finite; a program needn't handle non-finite values.
Results may differ from the reference program's by a relative error of at most 0.00018.
Values sent between devices are 32-bit elements; how exact they have to be, the bound alone decides.
A program may use at most 64 MiB of HBM per device.

```python
import math
import jax
import jax.numpy as jnp
from jax import lax

NT = 1024
LAGS = 15
TWIN = 12
HMAX = 3
WINLEN = 32
KW = 4
KSTEP = 8
XL_DEV = 16
NIL = 16
NXL = 128
NWIN = 32
SLABS = 8


def make_pair(key):
    base_key = jax.random.fold_in(key, 4242)
    key_raw = jax.random.fold_in(base_key, 1)
    key_lag = jax.random.fold_in(base_key, 2)
    key_trace = jax.random.fold_in(base_key, 3)
    key_envelope = jax.random.fold_in(base_key, 4)
    key_noise = jax.random.fold_in(base_key, 5)
    raw = jnp.clip(jax.random.normal(key_raw, (NIL, NXL, NT + 2 * LAGS), jnp.float32), -6.0, 6.0)
    noise = 0.5 * jnp.clip(jax.random.normal(key_noise, (NIL, NXL, NT), jnp.float32), -6.0, 6.0)
    lagging = jax.random.randint(key_lag, (NIL, NXL, 1), -7, 8)
    index_at = jnp.arange(NT)[None, None, :] + LAGS + lagging
    shifted = jnp.take_along_axis(raw, index_at, 2)
    drawn = raw[:, :, LAGS:LAGS + NT]
    trace_scale = jnp.exp(jax.random.uniform(key_trace, (NIL, NXL, 1), jnp.float32, 0.0, math.log(10.0)))
    blocks = jnp.exp(jax.random.uniform(key_envelope, (NIL, NXL, NT // 64), jnp.float32, 0.0, math.log(10.0)))
    envelope = jnp.repeat(blocks, 64, axis=2) * trace_scale / 10.0 * 10.0
    scaled = jnp.minimum(envelope, 100.0)
    return (drawn * scaled, (shifted + noise) * scaled)


def draw_baseline(key, part):
    return make_pair(key)[0]


def draw_monitor(key, part):
    return make_pair(key)[1]


def draw_knot_start(key, part):
    key_jitter = jax.random.fold_in(key, 77)
    jitter = jax.random.randint(key_jitter, (NWIN, KW), 0, 2)
    lowest = 0 - 3 * KSTEP // 2
    starts = KSTEP * jnp.arange(KW)[None, :] + lowest + jitter
    starts = starts.at[0, 0].set(lowest)
    starts = starts.at[0, KW - 1].set(KSTEP * (KW - 1) + lowest + 1)
    return starts.astype(jnp.int32)


def draw_half_width(key, part):
    key_values = jax.random.fold_in(key, 91)
    key_place = jax.random.fold_in(key, 92)
    widths = jax.random.randint(key_values, (SLABS,), 1, HMAX + 1)
    largest = jax.random.randint(key_place, (), 0, SLABS)
    widths = widths.at[largest].set(HMAX)
    widths = widths.at[(largest + 1) % SLABS].set(1)
    return widths.astype(jnp.int32)


def level_of(stream_key, extent, shards, low, high):
    def one(axis_at, shards_of):
        heights = jax.random.uniform(jax.random.fold_in(jax.random.fold_in(stream_key, 6), axis_at), (shards_of,), jnp.float32, low / len(shards), high / len(shards))
        return jnp.repeat(jnp.exp(heights), extent[axis_at] // shards_of).reshape((-1,) + (1,) * (len(extent) - axis_at - 1))

    gain = one(*shards[0])
    for cut in shards[1:]:
        gain = gain * one(*cut)
    return gain


def scatter_about(rng, dims, deviation, most, shards=(), held_as=jnp.bfloat16):
    values = jax.random.normal(rng, dims, jnp.float32) * deviation
    if len(shards) > 0:
        values = level_of(rng, dims, shards, -0.22, 0.18) * values
    return jnp.clip(values, min=-most, max=most).astype(held_as)


def setup_inputs(seed: int = 0) -> dict:
    key_of = jax.random.split(jax.random.key(seed), 6)
    return {
        "baseline": draw_baseline(jax.random.fold_in(key_of[5], 71), 0),
        "monitor": draw_monitor(jax.random.fold_in(key_of[5], 71), 0),
        "shift_model": scatter_about(key_of[2], (KW, NWIN, NXL), 1.0, 4.0, ((2, 8),), jnp.float32),
        "knot_start": draw_knot_start(jax.random.fold_in(key_of[5], 71), 0),
        "half_width": draw_half_width(jax.random.fold_in(key_of[5], 71), 0),
    }


EPSILON = 1e-06
SHARPNESS = 6.0
DAMPING = 0.5

def spline(offset):
    square = offset * offset
    cubed = square * offset
    piece_one = cubed / 6.0
    piece_two = (-3.0 * cubed + 12.0 * square - 12.0 * offset + 4.0) / 6.0
    piece_three = (3.0 * cubed - 24.0 * square + 60.0 * offset - 44.0) / 6.0
    remain = 4.0 - offset
    piece_four = remain * remain * remain / 6.0
    result = jnp.where(offset < 4.0, piece_four, 0.0 * offset)
    result = jnp.where(offset < 3.0, piece_three, result)
    result = jnp.where(offset < 2.0, piece_two, result)
    result = jnp.where(offset < 1.0, piece_one, result)
    return jnp.where(offset < 0.0, 0.0 * offset, result)

def basis_table(knot_start):
    positions = jnp.arange(WINLEN).astype(jnp.float32)
    offset = (positions[None, None, :] - knot_start[:, :, None].astype(jnp.float32)) / KSTEP
    return spline(offset)

def solve_small(matrix, target):
    lower = [[None] * KW for _ in range(KW)]
    for column in range(KW):
        pivot = matrix[column][column]
        for inner in range(column):
            pivot = pivot - lower[column][inner] * lower[column][inner]
        lower[column][column] = jnp.sqrt(pivot)
        for target_row in range(column + 1, KW):
            entry = matrix[target_row][column]
            for inner in range(column):
                entry = entry - lower[target_row][inner] * lower[column][inner]
            lower[target_row][column] = entry / lower[column][column]
    forward = []
    for column in range(KW):
        entry = target[column]
        for inner in range(column):
            entry = entry - lower[column][inner] * forward[inner]
        forward.append(entry / lower[column][column])
    backward = [None] * KW
    for column in range(KW - 1, -1, -1):
        entry = forward[column]
        for inner in range(column + 1, KW):
            entry = entry - lower[inner][column] * backward[inner]
        backward[column] = entry / lower[column][column]
    return jnp.stack(backward)

def box_time(values):
    samples = values.shape[2]
    width = 2 * TWIN + 1
    padded = jnp.pad(values, ((0, 0), (0, 0), (TWIN, TWIN)))
    partial_sums = {1: padded}
    length = 1
    while 2 * length <= width:
        previous = partial_sums[length]
        partial_sums[2 * length] = previous[:, :, :-length] + previous[:, :, length:]
        length = 2 * length
    total = None
    begin = 0
    remain = width
    while remain > 0:
        if length <= remain:
            piece = partial_sums[length][:, :, begin:begin + samples]
            total = piece if total is None else total + piece
            begin = begin + length
            remain = remain - length
        length = length // 2
    return total

def smooth(values, widths):
    timed = box_time(values)
    crossl = values.shape[1]
    sided = jnp.pad(timed, ((0, 0), (HMAX, HMAX), (0, 0)))
    total = None
    for offset in range(-HMAX, HMAX + 1):
        weight = (jnp.abs(offset) <= widths).astype(jnp.float32)[None, :, None]
        term = weight * sided[:, HMAX + offset:HMAX + offset + crossl]
        total = term if total is None else total + term
    return total

def reference(baseline, monitor, shift_model, knot_start, half_width):
    widths = jnp.repeat(half_width, XL_DEV)
    energy_base = smooth(baseline * baseline, widths)
    moni_pad = jnp.pad(monitor, ((0, 0), (0, 0), (LAGS, LAGS)))
    energy_mon = smooth(moni_pad * moni_pad, widths)
    total_exp = None
    for lag_value in range(-LAGS, LAGS + 1):
        lagged = moni_pad[:, :, LAGS + lag_value:LAGS + lag_value + NT]
        correlation = smooth(baseline * lagged, widths)
        energy = energy_mon[:, :, LAGS + lag_value:LAGS + lag_value + NT]
        normed = correlation / jnp.sqrt(energy_base * energy + EPSILON)
        weight_exp = jnp.exp(SHARPNESS * normed)
        if total_exp is None:
            total_exp = weight_exp
            total_shift = lag_value * weight_exp
            total_corr = normed * weight_exp
        else:
            total_exp = total_exp + weight_exp
            total_shift = total_shift + lag_value * weight_exp
            total_corr = total_corr + normed * weight_exp
    shift_obs = total_shift / total_exp
    confidence = 0.5 + 0.5 * total_corr / total_exp
    table = basis_table(knot_start)
    modelled = jnp.einsum('kwx,wku->xwu', shift_model, table, precision=lax.Precision.HIGHEST).reshape(NXL, NT)
    resid = shift_obs - modelled[None]
    resid_four = resid.reshape(NIL, NXL, NWIN, WINLEN)
    conf_four = confidence.reshape(NIL, NXL, NWIN, WINLEN)
    grad = jnp.einsum('ixwu,wku->kwx', conf_four * resid_four, table, precision=lax.Precision.HIGHEST)
    hess = jnp.einsum('ixwu,wku,wju->kjwx', conf_four, table, table, precision=lax.Precision.HIGHEST)
    matrix = [[hess[first_k, second_k] + (DAMPING * NIL if first_k == second_k else 0.0) for second_k in range(KW)] for first_k in range(KW)]
    target = [grad[first_k] for first_k in range(KW)]
    delta = solve_small(matrix, target)
    return (shift_obs, delta)
```

```python
import functools
import math

import jax
import jax.numpy as jnp
from jax import lax
from jax.experimental import pallas as pl
from jax.experimental.pallas import tpu as pltpu
from jax.sharding import PartitionSpec as P

LAGS = 15
TWIN = 12
HMAX = 3
WINLEN = 32
KW = 4
KSTEP = 8
EPSILON = 1e-06
SHARPNESS = 6.0
DAMPING = 0.5

LANES = 128
SUB = 8
REACH = LAGS + TWIN
NLAG = 2 * LAGS + 1
PAIRS = [(k, j) for k in range(KW) for j in range(k + 1)]
TERMS = KW + len(PAIRS)
MESH_ID = pl.DeviceIdType.MESH

TILES = 6
BLOCK = TILES * SUB
EVEN, ODD, ZERO = SUB, 3 * SUB, 5 * SUB
ENERGY = 3
SLOTS = ENERGY + NLAG
BASE_ROWS = WINLEN + 2 * TWIN
MONI_ROWS = WINLEN + 2 * REACH
HALO = [(1, 0), (1, 2), None, (0, 1), (1, 1), None, (0, 0), (0, 2)]
SCALE = SHARPNESS * math.log2(math.e)


def spline(offset):
    square = offset * offset
    cubed = square * offset
    piece_one = cubed / 6.0
    piece_two = (-3.0 * cubed + 12.0 * square - 12.0 * offset + 4.0) / 6.0
    piece_three = (3.0 * cubed - 24.0 * square + 60.0 * offset - 44.0) / 6.0
    remain = 4.0 - offset
    piece_four = remain * remain * remain / 6.0
    result = jnp.where(offset < 4.0, piece_four, 0.0 * offset)
    result = jnp.where(offset < 3.0, piece_three, result)
    result = jnp.where(offset < 2.0, piece_two, result)
    result = jnp.where(offset < 1.0, piece_one, result)
    return jnp.where(offset < 0.0, 0.0 * offset, result)


def box_sums(term, count, put):
    outs = -(-count // SUB)
    terms = {}

    def block(number):
        if number not in terms:
            terms[number] = [term(number * SUB + j) for j in range(SUB)]
        return terms[number]

    totals = {}
    suffixes = {}

    def total(number):
        if number not in totals:
            vals = block(number)
            while len(vals) > 1:
                vals = [vals[2 * j] + vals[2 * j + 1] for j in range(len(vals) // 2)]
            totals[number] = vals[0]
        return totals[number]

    def suffix(number):
        if number not in suffixes:
            vals = list(block(number))
            for j in range(SUB - 2, -1, -1):
                vals[j] = vals[j] + vals[j + 1]
            suffixes[number] = vals
            totals[number] = vals[0]
        return suffixes[number]

    for number in range(outs):
        tail = suffix(number)
        if number + 1 < outs:
            suffix(number + 1)
        if number + 2 < outs:
            suffix(number + 2)
        run = total(number + 1) + total(number + 2)
        for j in range(SUB):
            if number * SUB + j < count:
                position = (number + 3) * SUB + j
                if number + 3 in terms:
                    value = terms[number + 3][j]
                elif number + 3 < outs + 2:
                    value = block(number + 3)[j]
                else:
                    value = term(position)
                run = run + value
                put(number * SUB + j, tail[j] + run)


def trace_rows(i, x, width):
    return pl.ds((i * (width // SUB) + x // SUB) * SUB * SUB + x % SUB, SUB, stride=SUB)


def edge_tile(which, j, i, lines):
    return pl.ds(((which * HMAX + j) * lines + i) * SUB, SUB)


def swap_blocks(parts):
    block = lax.broadcasted_iota(jnp.int32, parts[0].shape, 1) // WINLEN
    low, even = block < 2, block % 2 == 0
    w, x, y, z = parts
    w, y = jnp.where(low, w, pltpu.roll(y, 64, 1)), jnp.where(low, pltpu.roll(w, 64, 1), y)
    x, z = jnp.where(low, x, pltpu.roll(z, 64, 1)), jnp.where(low, pltpu.roll(x, 64, 1), z)
    w, x = jnp.where(even, w, pltpu.roll(x, 32, 1)), jnp.where(even, pltpu.roll(w, 96, 1), x)
    y, z = jnp.where(even, y, pltpu.roll(z, 32, 1)), jnp.where(even, pltpu.roll(y, 96, 1), z)
    return [w, x, y, z]


def crossline(slot):
    return 2 * slot if slot < SUB else 2 * (slot - SUB) + 1


def step_kernel(
    groups, slabs, width, lines,
    half_ref, base_hbm, moni_hbm, coef_hbm, knot_hbm, shift_ref, total_ref,
    base_in, moni_in, coef_in, knot_in, edge, held, stage, wide, timed, ebase, emoni, table, model, acc, flat, mine, got,
    in_sem, halo_send, halo_recv, send_sem, recv_sem,
):
    row, col = lax.axis_index("inl"), lax.axis_index("xl")
    last = slabs - 1
    each = slabs // groups
    target_row = col // each
    place = row * each + col % each
    has_left, has_right = col > 0, col < last
    barrier = pltpu.get_barrier_semaphore()
    zeros = jnp.zeros((SUB, LANES), jnp.float32)

    loads = [
        pltpu.make_async_copy(src, dst, in_sem.at[number])
        for number, (src, dst) in enumerate(
            ((base_hbm, base_in), (moni_hbm, moni_in), (coef_hbm, coef_in), (knot_hbm, knot_in))
        )
    ]
    for load in loads:
        load.start()

    @pl.when(jnp.logical_not(has_left))
    def _():
        held[0] = jnp.zeros(held.shape[1:], jnp.float32)

    @pl.when(jnp.logical_not(has_right))
    def _():
        held[1] = jnp.zeros(held.shape[1:], jnp.float32)

    @pl.when(has_left)
    def _():
        pl.semaphore_signal(barrier, inc=1, device_id=(row, col - 1), device_id_type=MESH_ID)

    @pl.when(has_right)
    def _():
        pl.semaphore_signal(barrier, inc=1, device_id=(row, col + 1), device_id_type=MESH_ID)

    for step in range(slabs):
        source_row, source_col = step // each, row * each + step % each

        @pl.when(jnp.logical_or(source_row != row, source_col != col))
        def _():
            pl.semaphore_signal(
                barrier, inc=1, device_id=(source_row, source_col), device_id_type=MESH_ID
            )

    @pl.loop(0, SLOTS)
    def _(slot):
        for u in range(WINLEN):
            timed[u, slot, pl.ds(ZERO, SUB), :] = zeros

    loads[0].wait()
    loads[1].wait()

    for side, first in ((0, width - HMAX), (1, 0)):
        for which, ref in enumerate((base_in, moni_in)):
            for j in range(HMAX):
                for i in range(lines):
                    edge[side, edge_tile(which, j, i, lines), :] = ref[trace_rows(i, first + j, width), :]

    away = (row - target_row) * (row - target_row)
    greetings = slabs - 1 + (away + groups * groups - 1) // (groups * groups)
    greetings += (col + last) // slabs + (last - col + last) // slabs
    pl.semaphore_wait(barrier, greetings)

    def halo_copy(side, target):
        return pltpu.make_async_remote_copy(
            src_ref=edge.at[side],
            dst_ref=held.at[side],
            send_sem=halo_send.at[side],
            recv_sem=halo_recv.at[side],
            device_id=(row, target),
            device_id_type=MESH_ID,
        )

    @pl.when(has_right)
    def _():
        halo_copy(0, col + 1).start()

    @pl.when(has_left)
    def _():
        halo_copy(1, col - 1).start()

    lane = lax.broadcasted_iota(jnp.int32, (SUB, LANES), 1)
    block, tile = lane // WINLEN, lane % SUB
    not_first, not_last = block > 0, block < 3
    has_before, has_after = (tile > 0).astype(jnp.float32), (tile < SUB - 1).astype(jnp.float32)
    inputs = ((base_in, 0, TWIN), (moni_in, BASE_ROWS, REACH))

    def spread_parts(fetch, start, part_count, first_part):
        for which, (ref, origin, halo) in enumerate(inputs):
            for group in range(2 * part_count):
                parts = [
                    jnp.concatenate([fetch(which, ref, i, start + 4 * group + m) for i in range(lines)], axis=0)
                    for m in range(4)
                ]
                turned = jnp.concatenate(swap_blocks(parts), axis=0).T
                stage[which, pl.ds(group * LANES, LANES), :] = turned
            for u in range(WINLEN):
                for part in range(part_count):
                    band = pl.ds((first_part + part) * SUB, SUB)
                    value = stage[which, pl.ds(part * SUB * WINLEN + u, SUB, stride=WINLEN), :]
                    wide[origin + halo + u, band, :] = value
                    if u >= WINLEN - halo:
                        wide[origin + halo + u - WINLEN, band, :] = jnp.where(
                            not_first, pltpu.roll(value, 32, 1), pltpu.roll(value, 33, 1) * has_before
                        )
                    if u < halo:
                        wide[origin + halo + u + WINLEN, band, :] = jnp.where(
                            not_last, pltpu.roll(value, 96, 1), pltpu.roll(value, 95, 1) * has_after
                        )

    spread_parts(lambda which, ref, i, slot: ref[trace_rows(i, crossline(slot), width), :], 0, 2, 0)

    loads[2].wait()
    loads[3].wait()
    sample = lax.broadcasted_iota(jnp.int32, (WINLEN, LANES), 0).astype(jnp.float32)
    windows = knot_in.shape[1]
    window = lax.broadcasted_iota(jnp.int32, (windows, LANES), 0)
    column = lax.broadcasted_iota(jnp.int32, (windows, LANES), 1)
    pick = (window == 4 * (column % SUB) + column // WINLEN).astype(jnp.float32)

    def spread(values):
        return lax.dot_general(
            values, pick, (((1,), (0,)), ((), ())),
            precision=lax.Precision.HIGHEST, preferred_element_type=jnp.float32,
        )

    starts = spread(knot_in[...].astype(jnp.float32))
    phi = [spline((sample - starts[k : k + 1]) / KSTEP) for k in range(KW)]
    for k in range(KW):
        table[pl.ds(k, WINLEN, stride=2 * SUB), :] = phi[k]
        acc[k] = spread(coef_in[k])
        for part in range(2):
            model[k, pl.ds(part * SUB, SUB), :] = acc[k, pl.ds(part, SUB, stride=2), :]
    for number, (k, j) in enumerate(PAIRS):
        table[pl.ds(KW + number, WINLEN, stride=2 * SUB), :] = phi[k] * phi[j]

    def operands(slot):
        moni_energy = jnp.where(slot == 2, BASE_ROWS + 2 * LAGS, BASE_ROWS)
        is_moni = jnp.logical_or(slot == 1, slot == 2)
        first = jnp.where(is_moni, moni_energy, 0)
        second = jnp.where(slot == 0, 0, jnp.where(is_moni, moni_energy, BASE_ROWS + slot - ENERGY))
        return first, second

    @pl.loop(0, SLOTS)
    def _(slot):
        first, second = operands(slot)
        for part, offset in ((0, EVEN), (1, ODD)):
            band = pl.ds(part * SUB, SUB)

            def keep(u, value, offset=offset):
                timed[u, slot, pl.ds(offset, SUB), :] = value

            box_sums(lambda r, band=band: wide[first + r, band, :] * wide[second + r, band, :], WINLEN, keep)

    @pl.when(has_left)
    def _():
        pltpu.make_async_copy(edge.at[0], held.at[0], halo_recv.at[0]).wait()

    @pl.when(has_right)
    def _():
        pltpu.make_async_copy(edge.at[1], held.at[1], halo_recv.at[1]).wait()

    def halo_trace(which, ref, i, slot):
        if HALO[slot] is None:
            return zeros
        side, j = HALO[slot]
        return held[side, edge_tile(which, j, i, lines), :]

    spread_parts(halo_trace, 0, 1, 2)

    @pl.loop(0, SLOTS)
    def _(slot):
        first, second = operands(slot)
        band = pl.ds(2 * SUB, SUB)

        def keep(u, value):
            turned = pltpu.roll(value, 4, 0)
            timed[u, slot, pl.ds(0, SUB), :] = turned
            timed[u, slot, pl.ds(2 * SUB, SUB), :] = value
            timed[u, slot, pl.ds(4 * SUB, SUB), :] = turned

        box_sums(lambda r: wide[first + r, band, :] * wide[second + r, band, :], WINLEN, keep)

    half = half_ref[0]
    two, three = half >= 2, half >= 3
    near_odd = jnp.where(two, ODD - 1, ZERO)
    near_even = jnp.where(two, EVEN + 1, ZERO)
    far_even = jnp.where(three, EVEN - 1, ZERO)
    far_odd = jnp.where(three, ODD + 1, ZERO)
    end_even = jnp.where(three, ODD - 2, jnp.where(two, EVEN - 1, ODD - 1))
    end_odd = jnp.where(three, EVEN + 2, jnp.where(two, ODD + 1, EVEN + 1))

    def lateral(u, slot):
        def at(offset):
            return timed[u, slot, pl.ds(offset, SUB), :]

        middle = (at(EVEN) + at(ODD)) + (at(near_odd) + at(near_even)) + (at(far_even) + at(far_odd))
        return middle + at(end_even), middle + at(end_odd)

    @pl.loop(0, WINLEN)
    def _(u):
        for part, value in enumerate(lateral(u, 0)):
            ebase[u, pl.ds(part * SUB, SUB), :] = value * (1.0 / (SCALE * SCALE))
        for slot, shift in ((1, 0), (2, 2 * LAGS)):
            for part, value in enumerate(lateral(u, slot)):
                emoni[shift + u, pl.ds(part * SUB, SUB), :] = value

    acc[...] = jnp.zeros_like(acc)
    order = list(range(LAGS)) + list(range(2 * LAGS, LAGS, -1)) + [LAGS]

    @pl.loop(0, WINLEN)
    def _(u):
        energy_base = [ebase[u, pl.ds(part * SUB, SUB), :] for part in range(2)]
        run = [None, None]
        below = [None, None]
        moment = [None, None]
        corr = [None, None]
        for lag in order:
            sums = lateral(u, ENERGY + lag)
            for part in range(2):
                energy = energy_base[part] * emoni[u + lag, pl.ds(part * SUB, SUB), :]
                argument = sums[part] * lax.rsqrt(energy + EPSILON / (SCALE * SCALE))
                weight = jnp.exp2(argument)
                if lag == 2 * LAGS:
                    below[part], run[part] = run[part], None
                run[part] = weight if run[part] is None else run[part] + weight
                if lag != LAGS:
                    if moment[part] is None:
                        moment[part] = -run[part]
                    elif lag < LAGS:
                        moment[part] = moment[part] - run[part]
                    else:
                        moment[part] = moment[part] + run[part]
                product = argument * weight
                corr[part] = product if corr[part] is None else corr[part] + product
        for part in range(2):
            inverse = 1.0 / (below[part] + run[part])
            observed = moment[part] * inverse
            stage[0, pl.ds(part * SUB * WINLEN + u, SUB, stride=WINLEN), :] = observed
            conf = 0.5 + (0.5 / SCALE) * (corr[part] * inverse)
            band = pl.ds(part * SUB, SUB)
            basis = [table[pl.ds(u * 2 * SUB + k, 1), :] for k in range(TERMS)]
            tau = model[0, band, :] * basis[0]
            for k in range(1, KW):
                tau = tau + model[k, band, :] * basis[k]
            weighted = conf * (observed - tau)
            for k in range(TERMS):
                acc[k, band, :] += (weighted if k < KW else conf) * basis[k]

    for part in range(2):
        for k in range(TERMS):
            value = acc[k, pl.ds(part * SUB, SUB), :]
            value = value + pltpu.roll(value, LANES - SUB, 1)
            value = value + pltpu.roll(value, LANES - 2 * SUB, 1)
            flat[pl.ds(k * width + part, SUB, stride=2), :] = value
    spare = flat.shape[0] - TERMS * width
    if spare:
        flat[pl.ds(TERMS * width, spare), :] = jnp.zeros((spare, LANES), jnp.float32)
    turned = flat[...].T
    share = mine.shape[1]
    for owner in range(slabs):
        for j in range(share):
            number = owner * share + j
            lane_of = (number % 4) * WINLEN + number // 4
            mine[owner, j : j + 1] = turned[lane_of : lane_of + 1]

    def send(step):
        return pltpu.make_async_remote_copy(
            src_ref=mine.at[step],
            dst_ref=got.at[place],
            send_sem=send_sem.at[step],
            recv_sem=recv_sem.at[place],
            device_id=(target_row, step),
            device_id_type=MESH_ID,
        )

    for step in range(slabs):
        self_copy = jnp.logical_and(target_row == row, col == step)

        @pl.when(self_copy)
        def _():
            pltpu.make_async_copy(mine.at[col], got.at[place], recv_sem.at[place]).start()

        @pl.when(jnp.logical_not(self_copy))
        def _():
            send(step).start()

    for group in range(width // 4):
        back = stage[0, pl.ds(group * LANES, LANES), :].T
        parts = swap_blocks([back[WINLEN * m : WINLEN * (m + 1)] for m in range(4)])
        for m in range(4):
            for i in range(lines):
                rows = trace_rows(i, crossline(4 * group + m), width)
                shift_ref[rows, :] = parts[m][SUB * i : SUB * (i + 1)]

    for step in range(slabs):
        pltpu.make_async_copy(mine.at[0], got.at[step], recv_sem.at[step]).wait()
    for part in range(each):
        total = got[part]
        for group in range(1, groups):
            total = total + got[group * each + part]
        total_ref[part] = total

    for step in range(slabs):
        self_copy = jnp.logical_and(target_row == row, col == step)

        @pl.when(jnp.logical_not(self_copy))
        def _():
            send(step).wait_send()

    @pl.when(has_right)
    def _():
        halo_copy(0, col + 1).wait_send()

    @pl.when(has_left)
    def _():
        halo_copy(1, col - 1).wait_send()


def solve_small(matrix, target):
    lower = [[None] * KW for _ in range(KW)]
    for column in range(KW):
        pivot = matrix[column][column]
        for inner in range(column):
            pivot = pivot - lower[column][inner] * lower[column][inner]
        lower[column][column] = jnp.sqrt(pivot)
        for target_row in range(column + 1, KW):
            entry = matrix[target_row][column]
            for inner in range(column):
                entry = entry - lower[target_row][inner] * lower[column][inner]
            lower[target_row][column] = entry / lower[column][column]
    forward = []
    for column in range(KW):
        entry = target[column]
        for inner in range(column):
            entry = entry - lower[column][inner] * forward[inner]
        forward.append(entry / lower[column][column])
    backward = [None] * KW
    for column in range(KW - 1, -1, -1):
        entry = forward[column]
        for inner in range(column + 1, KW):
            entry = entry - lower[inner][column] * backward[inner]
        backward[column] = entry / lower[column][column]
    return backward


def finish_kernel(width, damping, shift_ref, total_ref, shift_out, delta_ref, sem):
    copy = pltpu.make_async_copy(shift_ref, shift_out, sem)
    copy.start()
    each, share = total_ref.shape[0], total_ref.shape[1]
    total = jnp.concatenate([total_ref[part] for part in range(each)], axis=0)

    def term(number):
        return total[:, number * width : (number + 1) * width]

    matrix = [[None] * KW for _ in range(KW)]
    for number, (k, j) in enumerate(PAIRS):
        matrix[k][j] = term(KW + number) + (damping if k == j else 0.0)
    delta = solve_small(matrix, [term(k) for k in range(KW)])
    for k in range(KW):
        for part in range(each):
            delta_ref[k, :, pl.ds(part * width, width)] = delta[k][part * share : (part + 1) * share]
    copy.wait()


def as_rows(block):
    lines, width, samples = block.shape
    tiles = block.reshape(lines, width // SUB, SUB, samples // LANES, LANES)
    return tiles.transpose(0, 1, 3, 2, 4).reshape(-1, LANES)


def from_rows(flat, lines, width, samples):
    tiles = flat.reshape(lines, width // SUB, samples // LANES, SUB, LANES)
    return tiles.transpose(0, 1, 3, 2, 4).reshape(lines, width, samples)


def per_device(baseline, monitor, shift_model, knot_start, half_width):
    lines, width, samples = baseline.shape
    windows = samples // WINLEN
    groups, slabs = lax.axis_size("inl"), lax.axis_size("xl")
    share, each = windows // slabs, slabs // groups
    packed = -(-(TERMS * width) // LANES) * LANES
    f32 = jnp.float32
    whole = pl.BlockSpec(memory_space=pltpu.VMEM)
    anywhere = pl.BlockSpec(memory_space=pl.ANY)
    base_rows, moni_rows = as_rows(baseline), as_rows(monitor)
    coef, knots = shift_model.transpose(0, 2, 1), knot_start.T
    edges = (2, 2 * HMAX * lines * SUB, LANES)
    dma = pltpu.SemaphoreType.DMA
    shift, total = pl.pallas_call(
        functools.partial(step_kernel, groups, slabs, width, lines),
        out_shape=(
            jax.ShapeDtypeStruct(base_rows.shape, f32),
            jax.ShapeDtypeStruct((each, share, packed), f32),
        ),
        in_specs=[pl.BlockSpec(memory_space=pltpu.SMEM)] + [anywhere] * 4,
        out_specs=(whole, whole),
        scratch_shapes=[
            pltpu.VMEM(base_rows.shape, f32),
            pltpu.VMEM(moni_rows.shape, f32),
            pltpu.VMEM(coef.shape, f32),
            pltpu.VMEM(knots.shape, jnp.int32),
            pltpu.VMEM(edges, f32),
            pltpu.VMEM(edges, f32),
            pltpu.VMEM((2, width * WINLEN, LANES), f32),
            pltpu.VMEM((BASE_ROWS + MONI_ROWS, 3 * SUB, LANES), f32),
            pltpu.VMEM((WINLEN, SLOTS, BLOCK, LANES), f32),
            pltpu.VMEM((WINLEN, width, LANES), f32),
            pltpu.VMEM((WINLEN + 2 * LAGS, width, LANES), f32),
            pltpu.VMEM((WINLEN * 2 * SUB, LANES), f32),
            pltpu.VMEM((KW, width, LANES), f32),
            pltpu.VMEM((TERMS, width, LANES), f32),
            pltpu.VMEM((packed, LANES), f32),
            pltpu.VMEM((slabs, share, packed), f32),
            pltpu.VMEM((slabs, share, packed), f32),
            dma((4,)),
            dma((2,)),
            dma((2,)),
            dma((slabs,)),
            dma((slabs,)),
        ],
        compiler_params=pltpu.CompilerParams(
            collective_id=0, has_side_effects=True, vmem_limit_bytes=48 * 1024 * 1024
        ),
        name="step",
    )(half_width, base_rows, moni_rows, coef, knots)
    shift, delta = pl.pallas_call(
        functools.partial(finish_kernel, width, DAMPING * lines * groups),
        out_shape=(
            jax.ShapeDtypeStruct(base_rows.shape, f32),
            jax.ShapeDtypeStruct((KW, share, each * width), f32),
        ),
        in_specs=[whole, whole],
        out_specs=(anywhere, whole),
        scratch_shapes=[dma],
        compiler_params=pltpu.CompilerParams(vmem_limit_bytes=8 * 1024 * 1024),
        name="finish",
    )(shift, total)
    return (from_rows(shift, lines, width, samples), delta)


def solution(mesh):
    in_specs = (P("inl", "xl", None), P("inl", "xl", None), P(None, None, "xl"), P(), P("xl"))
    out_specs = (P("inl", "xl", None), P(None, "xl", "inl"))
    return jax.shard_map(
        per_device, mesh=mesh, in_specs=in_specs, out_specs=out_specs, check_vma=False
    )
```

```python
import functools
import math

import jax
import jax.numpy as jnp
from jax import lax
from jax.experimental import pallas as pl
from jax.experimental.pallas import tpu as pltpu
from jax.sharding import PartitionSpec as P

LAGS = 15
TWIN = 12
HMAX = 3
WINLEN = 32
KW = 4
KSTEP = 8
EPSILON = 1e-06
SHARPNESS = 6.0
DAMPING = 0.5

LANES = 128
SUB = 8
REACH = LAGS + TWIN
NLAG = 2 * LAGS + 1
PAIRS = [(k, j) for k in range(KW) for j in range(k + 1)]
TERMS = KW + len(PAIRS)
MESH_ID = pl.DeviceIdType.MESH

TILES = 6
BLOCK = TILES * SUB
EVEN, ODD, ZERO = SUB, 3 * SUB, 5 * SUB
ENERGY = 3
SLOTS = ENERGY + NLAG
BASE_ROWS = WINLEN + 2 * TWIN
MONI_ROWS = WINLEN + 2 * REACH
HALO = [(1, 0), (1, 2), None, (0, 1), (1, 1), None, (0, 0), (0, 2)]
PITCH = WINLEN + 1
LINE = 2 * SUB + 1
SCALE = SHARPNESS * math.log2(math.e)


def spline(offset):
    square = offset * offset
    cubed = square * offset
    piece_one = cubed / 6.0
    piece_two = (-3.0 * cubed + 12.0 * square - 12.0 * offset + 4.0) / 6.0
    piece_three = (3.0 * cubed - 24.0 * square + 60.0 * offset - 44.0) / 6.0
    remain = 4.0 - offset
    piece_four = remain * remain * remain / 6.0
    result = jnp.where(offset < 4.0, piece_four, 0.0 * offset)
    result = jnp.where(offset < 3.0, piece_three, result)
    result = jnp.where(offset < 2.0, piece_two, result)
    result = jnp.where(offset < 1.0, piece_one, result)
    return jnp.where(offset < 0.0, 0.0 * offset, result)


def box_sums(term, count, put):
    outs = -(-count // SUB)
    terms = {}

    def block(number):
        if number not in terms:
            terms[number] = [term(number * SUB + j) for j in range(SUB)]
        return terms[number]

    totals = {}
    suffixes = {}

    def total(number):
        if number not in totals:
            vals = block(number)
            while len(vals) > 1:
                vals = [vals[2 * j] + vals[2 * j + 1] for j in range(len(vals) // 2)]
            totals[number] = vals[0]
        return totals[number]

    def suffix(number):
        if number not in suffixes:
            vals = list(block(number))
            for j in range(SUB - 2, -1, -1):
                vals[j] = vals[j] + vals[j + 1]
            suffixes[number] = vals
            totals[number] = vals[0]
        return suffixes[number]

    for number in range(outs):
        tail = suffix(number)
        if number + 1 < outs:
            suffix(number + 1)
        if number + 2 < outs:
            suffix(number + 2)
        run = total(number + 1) + total(number + 2)
        for j in range(SUB):
            if number * SUB + j < count:
                position = (number + 3) * SUB + j
                if number + 3 in terms:
                    value = terms[number + 3][j]
                elif number + 3 < outs + 2:
                    value = block(number + 3)[j]
                else:
                    value = term(position)
                run = run + value
                put(number * SUB + j, tail[j] + run)


def trace_rows(i, x, width):
    return pl.ds((i * (width // SUB) + x // SUB) * SUB * SUB + x % SUB, SUB, stride=SUB)


def edge_tile(which, j, i, lines):
    return pl.ds(((which * HMAX + j) * lines + i) * SUB, SUB)


def swap_blocks(parts):
    block = lax.broadcasted_iota(jnp.int32, parts[0].shape, 1) // WINLEN
    low, even = block < 2, block % 2 == 0
    w, x, y, z = parts
    w, y = jnp.where(low, w, pltpu.roll(y, 64, 1)), jnp.where(low, pltpu.roll(w, 64, 1), y)
    x, z = jnp.where(low, x, pltpu.roll(z, 64, 1)), jnp.where(low, pltpu.roll(x, 64, 1), z)
    w, x = jnp.where(even, w, pltpu.roll(x, 32, 1)), jnp.where(even, pltpu.roll(w, 96, 1), x)
    y, z = jnp.where(even, y, pltpu.roll(z, 32, 1)), jnp.where(even, pltpu.roll(y, 96, 1), z)
    return [w, x, y, z]


def crossline(slot):
    return 2 * slot if slot < SUB else 2 * (slot - SUB) + 1


def sums_kernel(
    width, lines,
    base_hbm, moni_hbm, coef_hbm, knot_hbm, timed, table, model,
    base_in, moni_in, coef_in, knot_in, edge, held, stage, wide, natural,
    in_sem, halo_send, halo_recv,
):
    row, col = lax.axis_index("inl"), lax.axis_index("xl")
    last = lax.axis_size("xl") - 1
    has_left, has_right = col > 0, col < last
    barrier = pltpu.get_barrier_semaphore()
    zeros = jnp.zeros((SUB, LANES), jnp.float32)

    loads = [
        pltpu.make_async_copy(src, dst, in_sem.at[number])
        for number, (src, dst) in enumerate(
            ((base_hbm, base_in), (moni_hbm, moni_in), (coef_hbm, coef_in), (knot_hbm, knot_in))
        )
    ]
    for load in loads:
        load.start()

    @pl.when(jnp.logical_not(has_left))
    def _():
        held[0] = jnp.zeros(held.shape[1:], jnp.float32)

    @pl.when(jnp.logical_not(has_right))
    def _():
        held[1] = jnp.zeros(held.shape[1:], jnp.float32)

    @pl.when(has_left)
    def _():
        pl.semaphore_signal(barrier, inc=1, device_id=(row, col - 1), device_id_type=MESH_ID)

    @pl.when(has_right)
    def _():
        pl.semaphore_signal(barrier, inc=1, device_id=(row, col + 1), device_id_type=MESH_ID)

    @pl.loop(0, SLOTS)
    def _(slot):
        for u in range(WINLEN):
            timed[u, slot, pl.ds(ZERO, SUB), :] = zeros

    loads[0].wait()
    loads[1].wait()

    for side, first in ((0, width - HMAX), (1, 0)):
        for which, ref in enumerate((base_in, moni_in)):
            for j in range(HMAX):
                for i in range(lines):
                    edge[side, edge_tile(which, j, i, lines), :] = ref[trace_rows(i, first + j, width), :]

    pl.semaphore_wait(barrier, (col + last) // (last + 1) + (last - col + last) // (last + 1))

    def halo_copy(side, target):
        return pltpu.make_async_remote_copy(
            src_ref=edge.at[side],
            dst_ref=held.at[side],
            send_sem=halo_send.at[side],
            recv_sem=halo_recv.at[side],
            device_id=(row, target),
            device_id_type=MESH_ID,
        )

    @pl.when(has_right)
    def _():
        halo_copy(0, col + 1).start()

    @pl.when(has_left)
    def _():
        halo_copy(1, col - 1).start()

    lane = lax.broadcasted_iota(jnp.int32, (SUB, LANES), 1)
    block, tile = lane // WINLEN, lane % SUB
    not_first, not_last = block > 0, block < 3
    has_before, has_after = (tile > 0).astype(jnp.float32), (tile < SUB - 1).astype(jnp.float32)
    inputs = ((base_in, 0, TWIN), (moni_in, BASE_ROWS, REACH))

    def spread_parts(fetch, start, part_count, first_part):
        for which, (ref, origin, halo) in enumerate(inputs):
            for group in range(2 * part_count):
                parts = [
                    jnp.concatenate([fetch(which, ref, i, start + 4 * group + m) for i in range(lines)], axis=0)
                    for m in range(4)
                ]
                turned = jnp.concatenate(swap_blocks(parts), axis=0).T
                for m in range(4):
                    stage[which, pl.ds((4 * group + m) * PITCH, WINLEN), :] = turned[m * WINLEN : (m + 1) * WINLEN]
            for u in range(WINLEN):
                for part in range(part_count):
                    band = pl.ds((first_part + part) * SUB, SUB)
                    value = stage[which, pl.ds(part * SUB * PITCH + u, SUB, stride=PITCH), :]
                    wide[origin + halo + u, band, :] = value
                    if u >= WINLEN - halo:
                        wide[origin + halo + u - WINLEN, band, :] = jnp.where(
                            not_first, pltpu.roll(value, 32, 1), pltpu.roll(value, 33, 1) * has_before
                        )
                    if u < halo:
                        wide[origin + halo + u + WINLEN, band, :] = jnp.where(
                            not_last, pltpu.roll(value, 96, 1), pltpu.roll(value, 95, 1) * has_after
                        )

    spread_parts(lambda which, ref, i, slot: ref[trace_rows(i, crossline(slot), width), :], 0, 2, 0)

    loads[2].wait()
    loads[3].wait()
    sample = lax.broadcasted_iota(jnp.int32, (WINLEN, LANES), 0).astype(jnp.float32)
    windows = knot_in.shape[1]
    window = lax.broadcasted_iota(jnp.int32, (windows, LANES), 0)
    column = lax.broadcasted_iota(jnp.int32, (windows, LANES), 1)
    pick = (window == 4 * (column % SUB) + column // WINLEN).astype(jnp.float32)

    def spread(values):
        return lax.dot_general(
            values, pick, (((1,), (0,)), ((), ())),
            precision=lax.Precision.HIGHEST, preferred_element_type=jnp.float32,
        )

    starts = spread(knot_in[...].astype(jnp.float32))
    phi = [spline((sample - starts[k : k + 1]) / KSTEP) for k in range(KW)]
    for k in range(KW):
        table[pl.ds(k, WINLEN, stride=LINE), :] = phi[k]
        natural[...] = spread(coef_in[k])
        for part in range(2):
            model[k, pl.ds(part * SUB, SUB), :] = natural[pl.ds(part, SUB, stride=2), :]
    for number, (k, j) in enumerate(PAIRS):
        table[pl.ds(KW + number, WINLEN, stride=LINE), :] = phi[k] * phi[j]

    def operands(slot):
        moni_energy = jnp.where(slot == 2, BASE_ROWS + 2 * LAGS, BASE_ROWS)
        is_moni = jnp.logical_or(slot == 1, slot == 2)
        first = jnp.where(is_moni, moni_energy, 0)
        second = jnp.where(slot == 0, 0, jnp.where(is_moni, moni_energy, BASE_ROWS + slot - ENERGY))
        return first, second

    @pl.loop(0, SLOTS, unroll=2)
    def _(slot):
        first, second = operands(slot)
        for part, offset in ((0, EVEN), (1, ODD)):
            band = pl.ds(part * SUB, SUB)

            def keep(u, value, offset=offset):
                timed[u, slot, pl.ds(offset, SUB), :] = value

            box_sums(lambda r, band=band: wide[first + r, band, :] * wide[second + r, band, :], WINLEN, keep)

    @pl.when(has_left)
    def _():
        pltpu.make_async_copy(edge.at[0], held.at[0], halo_recv.at[0]).wait()

    @pl.when(has_right)
    def _():
        pltpu.make_async_copy(edge.at[1], held.at[1], halo_recv.at[1]).wait()

    def halo_trace(which, ref, i, slot):
        if HALO[slot] is None:
            return zeros
        side, j = HALO[slot]
        return held[side, edge_tile(which, j, i, lines), :]

    spread_parts(halo_trace, 0, 1, 2)

    @pl.loop(0, SLOTS, unroll=2)
    def _(slot):
        first, second = operands(slot)
        band = pl.ds(2 * SUB, SUB)

        def keep(u, value):
            turned = pltpu.roll(value, 4, 0)
            timed[u, slot, pl.ds(0, SUB), :] = turned
            timed[u, slot, pl.ds(2 * SUB, SUB), :] = value
            timed[u, slot, pl.ds(4 * SUB, SUB), :] = turned

        box_sums(lambda r: wide[first + r, band, :] * wide[second + r, band, :], WINLEN, keep)

    @pl.when(has_right)
    def _():
        halo_copy(0, col + 1).wait_send()

    @pl.when(has_left)
    def _():
        halo_copy(1, col - 1).wait_send()


def lags_kernel(
    groups, slabs, width, lines,
    half_ref, timed, table, model, shift_ref, total_ref,
    stage, ebase, emoni, acc, flat, mine, got, send_sem, recv_sem,
):
    row, col = lax.axis_index("inl"), lax.axis_index("xl")
    each = slabs // groups
    target_row = col // each
    place = row * each + col % each
    barrier = pltpu.get_barrier_semaphore()
    for step in range(slabs):
        source_row, source_col = step // each, row * each + step % each

        @pl.when(jnp.logical_or(source_row != row, source_col != col))
        def _():
            pl.semaphore_signal(
                barrier, inc=1, device_id=(source_row, source_col), device_id_type=MESH_ID
            )

    half = half_ref[0]
    two, three = half >= 2, half >= 3
    near_odd = jnp.where(two, ODD - 1, ZERO)
    near_even = jnp.where(two, EVEN + 1, ZERO)
    far_even = jnp.where(three, EVEN - 1, ZERO)
    far_odd = jnp.where(three, ODD + 1, ZERO)
    end_even = jnp.where(three, ODD - 2, jnp.where(two, EVEN - 1, ODD - 1))
    end_odd = jnp.where(three, EVEN + 2, jnp.where(two, ODD + 1, EVEN + 1))

    def lateral(u, slot):
        def at(offset):
            return timed[u, slot, pl.ds(offset, SUB), :]

        middle = (at(EVEN) + at(ODD)) + (at(near_odd) + at(near_even)) + (at(far_even) + at(far_odd))
        return middle + at(end_even), middle + at(end_odd)

    @pl.loop(0, WINLEN)
    def _(u):
        for part, value in enumerate(lateral(u, 0)):
            ebase[u, pl.ds(part * SUB, SUB), :] = value * (1.0 / (SCALE * SCALE))
        for slot, shift in ((1, 0), (2, 2 * LAGS)):
            for part, value in enumerate(lateral(u, slot)):
                emoni[shift + u, pl.ds(part * SUB, SUB), :] = value

    acc[...] = jnp.zeros_like(acc)
    order = list(range(LAGS)) + list(range(2 * LAGS, LAGS, -1)) + [LAGS]

    @pl.loop(0, WINLEN)
    def _(u):
        energy_base = [ebase[u, pl.ds(part * SUB, SUB), :] for part in range(2)]
        run = [None, None]
        below = [None, None]
        moment = [None, None]
        corr = [None, None]
        for lag in order:
            sums = lateral(u, ENERGY + lag)
            for part in range(2):
                energy = energy_base[part] * emoni[u + lag, pl.ds(part * SUB, SUB), :]
                argument = sums[part] * lax.rsqrt(energy + EPSILON / (SCALE * SCALE))
                weight = jnp.exp2(argument)
                if lag == 2 * LAGS:
                    below[part], run[part] = run[part], None
                run[part] = weight if run[part] is None else run[part] + weight
                if lag != LAGS:
                    if moment[part] is None:
                        moment[part] = -run[part]
                    elif lag < LAGS:
                        moment[part] = moment[part] - run[part]
                    else:
                        moment[part] = moment[part] + run[part]
                product = argument * weight
                corr[part] = product if corr[part] is None else corr[part] + product
        for part in range(2):
            inverse = 1.0 / (below[part] + run[part])
            observed = moment[part] * inverse
            stage[pl.ds(part * SUB * PITCH + u, SUB, stride=PITCH), :] = observed
            conf = 0.5 + (0.5 / SCALE) * (corr[part] * inverse)
            band = pl.ds(part * SUB, SUB)
            basis = [table[pl.ds(u * LINE + k, 1), :] for k in range(TERMS)]
            tau = model[0, band, :] * basis[0]
            for k in range(1, KW):
                tau = tau + model[k, band, :] * basis[k]
            weighted = conf * (observed - tau)
            for k in range(TERMS):
                acc[k, band, :] += (weighted if k < KW else conf) * basis[k]

    for part in range(2):
        for k in range(TERMS):
            value = acc[k, pl.ds(part * SUB, SUB), :]
            value = value + pltpu.roll(value, LANES - SUB, 1)
            value = value + pltpu.roll(value, LANES - 2 * SUB, 1)
            flat[pl.ds(k * width + part, SUB, stride=2), :] = value
    spare = flat.shape[0] - TERMS * width
    if spare:
        flat[pl.ds(TERMS * width, spare), :] = jnp.zeros((spare, LANES), jnp.float32)
    turned = flat[...].T
    share = mine.shape[1]
    for owner in range(slabs):
        for j in range(share):
            number = owner * share + j
            lane_of = (number % 4) * WINLEN + number // 4
            mine[owner, j : j + 1] = turned[lane_of : lane_of + 1]

    def send(step):
        return pltpu.make_async_remote_copy(
            src_ref=mine.at[step],
            dst_ref=got.at[place],
            send_sem=send_sem.at[step],
            recv_sem=recv_sem.at[place],
            device_id=(target_row, step),
            device_id_type=MESH_ID,
        )

    away = (row - target_row) * (row - target_row)
    pl.semaphore_wait(barrier, slabs - 1 + (away + groups * groups - 1) // (groups * groups))
    for step in range(slabs):
        self_copy = jnp.logical_and(target_row == row, col == step)

        @pl.when(self_copy)
        def _():
            pltpu.make_async_copy(mine.at[col], got.at[place], recv_sem.at[place]).start()

        @pl.when(jnp.logical_not(self_copy))
        def _():
            send(step).start()

    for group in range(width // 4):
        back = jnp.concatenate(
            [stage[pl.ds((4 * group + m) * PITCH, WINLEN), :] for m in range(4)], axis=0
        ).T
        parts = swap_blocks([back[WINLEN * m : WINLEN * (m + 1)] for m in range(4)])
        for m in range(4):
            for i in range(lines):
                rows = trace_rows(i, crossline(4 * group + m), width)
                shift_ref[rows, :] = parts[m][SUB * i : SUB * (i + 1)]

    for step in range(slabs):
        pltpu.make_async_copy(mine.at[0], got.at[step], recv_sem.at[step]).wait()
    for part in range(each):
        total = got[part]
        for group in range(1, groups):
            total = total + got[group * each + part]
        total_ref[part] = total

    for step in range(slabs):
        self_copy = jnp.logical_and(target_row == row, col == step)

        @pl.when(jnp.logical_not(self_copy))
        def _():
            send(step).wait_send()


def solve_small(matrix, target):
    lower = [[None] * KW for _ in range(KW)]
    for column in range(KW):
        pivot = matrix[column][column]
        for inner in range(column):
            pivot = pivot - lower[column][inner] * lower[column][inner]
        lower[column][column] = jnp.sqrt(pivot)
        for target_row in range(column + 1, KW):
            entry = matrix[target_row][column]
            for inner in range(column):
                entry = entry - lower[target_row][inner] * lower[column][inner]
            lower[target_row][column] = entry / lower[column][column]
    forward = []
    for column in range(KW):
        entry = target[column]
        for inner in range(column):
            entry = entry - lower[column][inner] * forward[inner]
        forward.append(entry / lower[column][column])
    backward = [None] * KW
    for column in range(KW - 1, -1, -1):
        entry = forward[column]
        for inner in range(column + 1, KW):
            entry = entry - lower[inner][column] * backward[inner]
        backward[column] = entry / lower[column][column]
    return backward


def finish_kernel(width, damping, shift_ref, total_ref, shift_out, delta_ref, sem):
    copy = pltpu.make_async_copy(shift_ref, shift_out, sem)
    copy.start()
    each, share = total_ref.shape[0], total_ref.shape[1]
    total = jnp.concatenate([total_ref[part] for part in range(each)], axis=0)

    def term(number):
        return total[:, number * width : (number + 1) * width]

    matrix = [[None] * KW for _ in range(KW)]
    for number, (k, j) in enumerate(PAIRS):
        matrix[k][j] = term(KW + number) + (damping if k == j else 0.0)
    delta = solve_small(matrix, [term(k) for k in range(KW)])
    for k in range(KW):
        for part in range(each):
            delta_ref[k, :, pl.ds(part * width, width)] = delta[k][part * share : (part + 1) * share]
    copy.wait()


def as_rows(block):
    lines, width, samples = block.shape
    tiles = block.reshape(lines, width // SUB, SUB, samples // LANES, LANES)
    return tiles.transpose(0, 1, 3, 2, 4).reshape(-1, LANES)


def from_rows(flat, lines, width, samples):
    tiles = flat.reshape(lines, width // SUB, samples // LANES, SUB, LANES)
    return tiles.transpose(0, 1, 3, 2, 4).reshape(lines, width, samples)


def per_device(baseline, monitor, shift_model, knot_start, half_width):
    lines, width, samples = baseline.shape
    windows = samples // WINLEN
    groups, slabs = lax.axis_size("inl"), lax.axis_size("xl")
    share, each = windows // slabs, slabs // groups
    packed = -(-(TERMS * width) // LANES) * LANES
    f32 = jnp.float32
    whole = pl.BlockSpec(memory_space=pltpu.VMEM)
    anywhere = pl.BlockSpec(memory_space=pltpu.HBM)
    base_rows, moni_rows = as_rows(baseline), as_rows(monitor)
    coef, knots = shift_model.transpose(0, 2, 1), knot_start.T
    base_rows, moni_rows, coef, knots = (
        pltpu.with_memory_space_constraint(value, pltpu.HBM) for value in (base_rows, moni_rows, coef, knots)
    )
    edges = (2, 2 * HMAX * lines * SUB, LANES)
    dma = pltpu.SemaphoreType.DMA
    timed, table, model = pl.pallas_call(
        functools.partial(sums_kernel, width, lines),
        out_shape=(
            jax.ShapeDtypeStruct((WINLEN, SLOTS, BLOCK, LANES), f32),
            jax.ShapeDtypeStruct((WINLEN * LINE, LANES), f32),
            jax.ShapeDtypeStruct((KW, width, LANES), f32),
        ),
        in_specs=[anywhere] * 4,
        out_specs=(whole,) * 3,
        scratch_shapes=[
            pltpu.VMEM(base_rows.shape, f32),
            pltpu.VMEM(moni_rows.shape, f32),
            pltpu.VMEM(coef.shape, f32),
            pltpu.VMEM(knots.shape, jnp.int32),
            pltpu.VMEM(edges, f32),
            pltpu.VMEM(edges, f32),
            pltpu.VMEM((2, width * PITCH, LANES), f32),
            pltpu.VMEM((BASE_ROWS + MONI_ROWS, 3 * SUB, LANES), f32),
            pltpu.VMEM((width, LANES), f32),
            dma((4,)),
            dma((2,)),
            dma((2,)),
        ],
        compiler_params=pltpu.CompilerParams(
            collective_id=1, has_side_effects=True, vmem_limit_bytes=12 * 1024 * 1024
        ),
        name="sums",
    )(base_rows, moni_rows, coef, knots)
    shift, total = pl.pallas_call(
        functools.partial(lags_kernel, groups, slabs, width, lines),
        out_shape=(
            jax.ShapeDtypeStruct(base_rows.shape, f32),
            jax.ShapeDtypeStruct((each, share, packed), f32),
        ),
        in_specs=[pl.BlockSpec(memory_space=pltpu.SMEM)] + [whole] * 3,
        out_specs=(whole, whole),
        scratch_shapes=[
            pltpu.VMEM((width * PITCH, LANES), f32),
            pltpu.VMEM((WINLEN, width, LANES), f32),
            pltpu.VMEM((WINLEN + 2 * LAGS, width, LANES), f32),
            pltpu.VMEM((TERMS, width, LANES), f32),
            pltpu.VMEM((packed, LANES), f32),
            pltpu.VMEM((slabs, share, packed), f32),
            pltpu.VMEM((slabs, share, packed), f32),
            dma((slabs,)),
            dma((slabs,)),
        ],
        compiler_params=pltpu.CompilerParams(
            collective_id=0, has_side_effects=True, vmem_limit_bytes=12 * 1024 * 1024
        ),
        name="lags",
    )(half_width, timed, table, model)
    shift, delta = pl.pallas_call(
        functools.partial(finish_kernel, width, DAMPING * lines * groups),
        out_shape=(
            jax.ShapeDtypeStruct(base_rows.shape, f32),
            jax.ShapeDtypeStruct((KW, share, each * width), f32),
        ),
        in_specs=[whole, whole],
        out_specs=(anywhere, whole),
        scratch_shapes=[dma],
        compiler_params=pltpu.CompilerParams(vmem_limit_bytes=8 * 1024 * 1024),
        name="finish",
    )(shift, total)
    return (from_rows(shift, lines, width, samples), delta)


def solution(mesh):
    in_specs = (P("inl", "xl", None), P("inl", "xl", None), P(None, None, "xl"), P(), P("xl"))
    out_specs = (P("inl", "xl", None), P(None, "xl", "inl"))
    return jax.shard_map(
        per_device, mesh=mesh, in_specs=in_specs, out_specs=out_specs, check_vma=False
    )
```

```python
import functools
import math

import jax
import jax.numpy as jnp
from jax import lax
from jax.experimental import pallas as pl
from jax.experimental.pallas import tpu as pltpu
from jax.sharding import PartitionSpec as P

LAGS = 15
TWIN = 12
HMAX = 3
WINLEN = 32
KW = 4
KSTEP = 8
EPSILON = 1e-06
SHARPNESS = 6.0
DAMPING = 0.5

LANES = 128
SUB = 8
REACH = LAGS + TWIN
NLAG = 2 * LAGS + 1
PAIRS = [(k, j) for k in range(KW) for j in range(k + 1)]
TERMS = KW + len(PAIRS)
MESH_ID = pl.DeviceIdType.MESH

TILES = 6
BLOCK = TILES * SUB
EVEN, ODD, ZERO = SUB, 3 * SUB, 5 * SUB
ENERGY = 3
SLOTS = ENERGY + NLAG
STEP = SLOTS * BLOCK + SUB
BASE_ROWS = WINLEN + 2 * TWIN
MONI_ROWS = WINLEN + 2 * REACH
HALO = [(1, 0), (1, 2), None, (0, 1), (1, 1), None, (0, 0), (0, 2)]
PITCH = WINLEN + 1
LINE = 2 * SUB + 1
SCALE = SHARPNESS * math.log2(math.e)


def spline(offset):
    square = offset * offset
    cubed = square * offset
    piece_one = cubed / 6.0
    piece_two = (-3.0 * cubed + 12.0 * square - 12.0 * offset + 4.0) / 6.0
    piece_three = (3.0 * cubed - 24.0 * square + 60.0 * offset - 44.0) / 6.0
    remain = 4.0 - offset
    piece_four = remain * remain * remain / 6.0
    result = jnp.where(offset < 4.0, piece_four, 0.0 * offset)
    result = jnp.where(offset < 3.0, piece_three, result)
    result = jnp.where(offset < 2.0, piece_two, result)
    result = jnp.where(offset < 1.0, piece_one, result)
    return jnp.where(offset < 0.0, 0.0 * offset, result)


def plus(left, right):
    return tuple(x + y for x, y in zip(left, right))


def box_sums(term, put):
    outs = WINLEN // SUB
    terms, totals, suffixes = {}, {}, {}

    def block(number):
        if number not in terms:
            terms[number] = [term(number * SUB + j) for j in range(SUB)]
        return terms[number]

    def suffix(number):
        if number not in suffixes:
            vals = list(block(number))
            for j in range(SUB - 2, -1, -1):
                vals[j] = plus(vals[j], vals[j + 1])
            suffixes[number] = vals
            totals[number] = vals[0]
        return suffixes[number]

    def total(number):
        if number not in totals:
            vals = block(number)
            while len(vals) > 1:
                vals = [plus(vals[2 * j], vals[2 * j + 1]) for j in range(len(vals) // 2)]
            totals[number] = vals[0]
        return totals[number]

    for number in range(outs):
        tail = suffix(number)
        for later in (number + 1, number + 2):
            if later < outs:
                suffix(later)
        run = plus(total(number + 1), total(number + 2))
        for j in range(SUB):
            value = block(number + 3)[j] if number + 3 < outs + 2 else term((number + 3) * SUB + j)
            run = plus(run, value)
            put(number * SUB + j, plus(tail[j], run))


def trace_rows(i, x, width):
    return pl.ds((i * (width // SUB) + x // SUB) * SUB * SUB + x % SUB, SUB, stride=SUB)


def edge_tile(j, i, lines):
    return pl.ds((j * lines + i) * SUB, SUB)


def swap_blocks(parts):
    block = lax.broadcasted_iota(jnp.int32, parts[0].shape, 1) // WINLEN
    low, even = block < 2, block % 2 == 0
    w, x, y, z = parts
    w, y = jnp.where(low, w, pltpu.roll(y, 64, 1)), jnp.where(low, pltpu.roll(w, 64, 1), y)
    x, z = jnp.where(low, x, pltpu.roll(z, 64, 1)), jnp.where(low, pltpu.roll(x, 64, 1), z)
    w, x = jnp.where(even, w, pltpu.roll(x, 32, 1)), jnp.where(even, pltpu.roll(w, 96, 1), x)
    y, z = jnp.where(even, y, pltpu.roll(z, 32, 1)), jnp.where(even, pltpu.roll(y, 96, 1), z)
    return [w, x, y, z]


def crossline(slot):
    return 2 * slot if slot < SUB else 2 * (slot - SUB) + 1


def sums_kernel(
    width, lines,
    base_hbm, moni_hbm, coef_hbm, knot_hbm, timed, table, model,
    base_in, moni_in, coef_in, knot_in, edge, held, stage, wide, natural,
    in_sem, halo_send, halo_recv,
):
    row, col = lax.axis_index("inl"), lax.axis_index("xl")
    last = lax.axis_size("xl") - 1
    has_left, has_right = col > 0, col < last
    barrier = pltpu.get_barrier_semaphore()
    zeros = jnp.zeros((SUB, LANES), jnp.float32)

    loads = [
        pltpu.make_async_copy(src, dst, in_sem.at[number])
        for number, (src, dst) in enumerate(
            ((base_hbm, base_in), (moni_hbm, moni_in), (coef_hbm, coef_in), (knot_hbm, knot_in))
        )
    ]
    @pl.when(has_left)
    def _():
        pl.semaphore_signal(barrier, inc=1, device_id=(row, col - 1), device_id_type=MESH_ID)

    @pl.when(has_right)
    def _():
        pl.semaphore_signal(barrier, inc=1, device_id=(row, col + 1), device_id_type=MESH_ID)

    for load in loads:
        load.start()

    @pl.when(jnp.logical_not(has_left))
    def _():
        held[0] = jnp.zeros(held.shape[1:], jnp.float32)

    @pl.when(jnp.logical_not(has_right))
    def _():
        held[1] = jnp.zeros(held.shape[1:], jnp.float32)

    @pl.loop(0, SLOTS)
    def _(slot):
        for u in range(WINLEN):
            timed[pl.ds(u * STEP + slot * BLOCK + ZERO, SUB), :] = zeros

    loads[0].wait()
    loads[1].wait()

    for side, first in ((0, width - HMAX), (1, 0)):
        for which, ref in enumerate((base_in, moni_in)):
            for j in range(HMAX):
                for i in range(lines):
                    edge[side, which, edge_tile(j, i, lines), :] = ref[trace_rows(i, first + j, width), :]

    pl.semaphore_wait(barrier, (col + last) // (last + 1) + (last - col + last) // (last + 1))

    def halo_copy(side, which):
        return pltpu.make_async_remote_copy(
            src_ref=edge.at[side, which],
            dst_ref=held.at[side, which],
            send_sem=halo_send.at[side, which],
            recv_sem=halo_recv.at[side, which],
            device_id=(row, col + 1 if side == 0 else col - 1),
            device_id_type=MESH_ID,
        )

    def halo_wait(which):
        for side, here in ((0, has_left), (1, has_right)):

            @pl.when(here)
            def _(side=side):
                pltpu.make_async_copy(edge.at[side, which], held.at[side, which], halo_recv.at[side, which]).wait()

    for which in (1, 0):
        for side, there in ((0, has_right), (1, has_left)):

            @pl.when(there)
            def _(side=side, which=which):
                halo_copy(side, which).start()

    lane = lax.broadcasted_iota(jnp.int32, (SUB, LANES), 1)
    block, tile = lane // WINLEN, lane % SUB
    not_first, not_last = block > 0, block < 3
    has_before, has_after = (tile > 0).astype(jnp.float32), (tile < SUB - 1).astype(jnp.float32)
    inputs = ((base_in, 0, TWIN), (moni_in, BASE_ROWS, REACH))

    def spread_parts(fetch, start, part_count, first_part):
        for which, (ref, origin, halo) in ((1, inputs[1]), (0, inputs[0])):
            if first_part:
                halo_wait(which)
            for group in range(2 * part_count):
                parts = [
                    jnp.concatenate([fetch(which, ref, i, start + 4 * group + m) for i in range(lines)], axis=0)
                    for m in range(4)
                ]
                turned = jnp.concatenate(swap_blocks(parts), axis=0).T
                for m in range(4):
                    stage[which, pl.ds((4 * group + m) * PITCH, WINLEN), :] = turned[m * WINLEN : (m + 1) * WINLEN]
            for u in range(WINLEN):
                for part in range(part_count):
                    band = pl.ds((first_part + part) * SUB, SUB)
                    value = stage[which, pl.ds(part * SUB * PITCH + u, SUB, stride=PITCH), :]
                    wide[origin + halo + u, band, :] = value
                    if u >= WINLEN - halo:
                        wide[origin + halo + u - WINLEN, band, :] = jnp.where(
                            not_first, pltpu.roll(value, 32, 1), pltpu.roll(value, 33, 1) * has_before
                        )
                    if u < halo:
                        wide[origin + halo + u + WINLEN, band, :] = jnp.where(
                            not_last, pltpu.roll(value, 96, 1), pltpu.roll(value, 95, 1) * has_after
                        )

    spread_parts(lambda which, ref, i, slot: ref[trace_rows(i, crossline(slot), width), :], 0, 2, 0)

    loads[2].wait()
    loads[3].wait()
    sample = lax.broadcasted_iota(jnp.int32, (WINLEN, LANES), 0).astype(jnp.float32)
    windows = knot_in.shape[1]
    window = lax.broadcasted_iota(jnp.int32, (windows, LANES), 0)
    column = lax.broadcasted_iota(jnp.int32, (windows, LANES), 1)
    pick = (window == 4 * (column % SUB) + column // WINLEN).astype(jnp.float32)

    def spread(values):
        return lax.dot_general(
            values, pick, (((1,), (0,)), ((), ())),
            precision=lax.Precision.HIGHEST, preferred_element_type=jnp.float32,
        )

    starts = spread(knot_in[...].astype(jnp.float32))
    phi = [spline((sample - starts[k : k + 1]) / KSTEP) for k in range(KW)]
    for k in range(KW):
        table[pl.ds(k, WINLEN, stride=LINE), :] = phi[k]
        natural[...] = spread(coef_in[k])
        for part in range(2):
            model[k, pl.ds(part * SUB, SUB), :] = natural[pl.ds(part, SUB, stride=2), :]
    for number, (k, j) in enumerate(PAIRS):
        table[pl.ds(KW + number, WINLEN, stride=LINE), :] = phi[k] * phi[j]

    def operands(slot):
        moni_energy = jnp.where(slot == 2, BASE_ROWS + 2 * LAGS, BASE_ROWS)
        is_moni = jnp.logical_or(slot == 1, slot == 2)
        first = jnp.where(is_moni, moni_energy, 0)
        second = jnp.where(slot == 0, 0, jnp.where(is_moni, moni_energy, BASE_ROWS + slot - ENERGY))
        return first, second

    def each_slot(tile, keep):
        band = pl.ds(tile * SUB, SUB)

        def single(slot):
            first, second = operands(slot)

            def term(r):
                return (wide[first + r, band, :] * wide[second + r, band, :],)

            def put(u, values):
                keep(u, slot, values[0])

            box_sums(term, put)

        def double(slot):
            moni = BASE_ROWS + slot - ENERGY
            rows = {}

            def row(r):
                if r not in rows:
                    rows[r] = wide[moni + r, band, :]
                return rows[r]

            def term(r):
                value = wide[r, band, :]
                return (value * row(r), value * row(r + 1))

            def put(u, values):
                keep(u, slot, values[0])
                keep(u, slot + 1, values[1])

            box_sums(term, put)

        return single, double

    def own_keep(offset):
        def keep(u, slot, value):
            timed[pl.ds(u * STEP + slot * BLOCK + offset, SUB), :] = value

        return keep

    own = [each_slot(0, own_keep(EVEN)), each_slot(1, own_keep(ODD))]

    @pl.loop(0, ENERGY + 1)
    def _(number):
        for single, _ in own:
            single(jnp.where(number < ENERGY, number, SLOTS - 1))

    @pl.loop(0, LAGS)
    def _(number):
        for _, double in own:
            double(ENERGY + 2 * number)

    def halo_trace(which, ref, i, slot):
        if HALO[slot] is None:
            return zeros
        side, j = HALO[slot]
        return held[side, which, edge_tile(j, i, lines), :]

    spread_parts(halo_trace, 0, 1, 2)

    def halo_keep(u, slot, value):
        place = u * STEP + slot * BLOCK
        timed[pl.ds(place + 4, 4), :] = value[0:4]
        timed[pl.ds(place + 2 * SUB, SUB), :] = value
        timed[pl.ds(place + 4 * SUB, 4), :] = value[4:8]

    single, double = each_slot(2, halo_keep)

    @pl.loop(0, ENERGY + 1, unroll=2)
    def _(number):
        single(jnp.where(number < ENERGY, number, SLOTS - 1))

    @pl.loop(0, LAGS)
    def _(number):
        double(ENERGY + 2 * number)

    for which in (1, 0):
        for side, there in ((0, has_right), (1, has_left)):

            @pl.when(there)
            def _(side=side, which=which):
                halo_copy(side, which).wait_send()


def lags_kernel(
    groups, slabs, width, lines,
    half_ref, timed, table, model, shift_ref, total_ref,
    stage, emoni, acc, flat, mine, got, send_sem, recv_sem,
):
    row, col = lax.axis_index("inl"), lax.axis_index("xl")
    each = slabs // groups
    target_row = col // each
    place = row * each + col % each
    barrier = pltpu.get_barrier_semaphore()
    for step in range(slabs):
        source_row, source_col = step // each, row * each + step % each

        @pl.when(jnp.logical_or(source_row != row, source_col != col))
        def _():
            pl.semaphore_signal(
                barrier, inc=1, device_id=(source_row, source_col), device_id_type=MESH_ID
            )

    half = half_ref[0]
    two, three = half >= 2, half >= 3
    near_odd = jnp.where(two, ODD - 1, ZERO)
    near_even = jnp.where(two, EVEN + 1, ZERO)
    far_even = jnp.where(three, EVEN - 1, ZERO)
    far_odd = jnp.where(three, ODD + 1, ZERO)
    end_even = jnp.where(three, ODD - 2, jnp.where(two, EVEN - 1, ODD - 1))
    end_odd = jnp.where(three, EVEN + 2, jnp.where(two, ODD + 1, EVEN + 1))

    def lateral(u, slot):
        def at(offset):
            return timed[pl.ds(u * STEP + slot * BLOCK + offset, SUB), :]

        middle = (at(EVEN) + at(ODD)) + (at(near_odd) + at(near_even)) + (at(far_even) + at(far_odd))
        return middle + at(end_even), middle + at(end_odd)

    @pl.loop(0, WINLEN, unroll=4)
    def _(u):
        for slot, shift in ((1, 0), (2, 2 * LAGS)):
            for part, value in enumerate(lateral(u, slot)):
                emoni[shift + u, pl.ds(part * SUB, SUB), :] = value

    acc[...] = jnp.zeros_like(acc)
    order = list(range(LAGS)) + list(range(2 * LAGS, LAGS, -1)) + [LAGS]

    @pl.loop(0, WINLEN, unroll=4)
    def _(u):
        energy_base = [value * (1.0 / (SCALE * SCALE)) for value in lateral(u, 0)]
        run = [None, None]
        below = [None, None]
        moment = [None, None]
        corr = [None, None]
        for lag in order:
            sums = lateral(u, ENERGY + lag)
            for part in range(2):
                energy = energy_base[part] * emoni[u + lag, pl.ds(part * SUB, SUB), :]
                argument = sums[part] * lax.rsqrt(energy + EPSILON / (SCALE * SCALE))
                weight = jnp.exp2(argument)
                if lag == 2 * LAGS:
                    below[part], run[part] = run[part], None
                run[part] = weight if run[part] is None else run[part] + weight
                if lag != LAGS:
                    if moment[part] is None:
                        moment[part] = -run[part]
                    elif lag < LAGS:
                        moment[part] = moment[part] - run[part]
                    else:
                        moment[part] = moment[part] + run[part]
                product = argument * weight
                corr[part] = product if corr[part] is None else corr[part] + product
        for part in range(2):
            inverse = 1.0 / (below[part] + run[part])
            observed = moment[part] * inverse
            stage[pl.ds(part * SUB * PITCH + u, SUB, stride=PITCH), :] = observed
            conf = 0.5 + (0.5 / SCALE) * (corr[part] * inverse)
            band = pl.ds(part * SUB, SUB)
            basis = [table[pl.ds(u * LINE + k, 1), :] for k in range(TERMS)]
            tau = model[0, band, :] * basis[0]
            for k in range(1, KW):
                tau = tau + model[k, band, :] * basis[k]
            weighted = conf * (observed - tau)
            for k in range(TERMS):
                acc[k, band, :] += (weighted if k < KW else conf) * basis[k]

    for part in range(2):
        for k in range(TERMS):
            value = acc[k, pl.ds(part * SUB, SUB), :]
            value = value + pltpu.roll(value, LANES - SUB, 1)
            value = value + pltpu.roll(value, LANES - 2 * SUB, 1)
            flat[pl.ds(k * width + part, SUB, stride=2), :] = value
    spare = flat.shape[0] - TERMS * width
    if spare:
        flat[pl.ds(TERMS * width, spare), :] = jnp.zeros((spare, LANES), jnp.float32)
    turned = flat[...].T
    share = mine.shape[1]
    for owner in range(slabs):
        for j in range(share):
            number = owner * share + j
            lane_of = (number % 4) * WINLEN + number // 4
            mine[owner, j : j + 1] = turned[lane_of : lane_of + 1]

    def send(step):
        return pltpu.make_async_remote_copy(
            src_ref=mine.at[step],
            dst_ref=got.at[place],
            send_sem=send_sem.at[step],
            recv_sem=recv_sem.at[place],
            device_id=(target_row, step),
            device_id_type=MESH_ID,
        )

    away = (row - target_row) * (row - target_row)
    pl.semaphore_wait(barrier, slabs - 1 + (away + groups * groups - 1) // (groups * groups))
    for step in range(slabs):
        self_copy = jnp.logical_and(target_row == row, col == step)

        @pl.when(self_copy)
        def _():
            pltpu.make_async_copy(mine.at[col], got.at[place], recv_sem.at[place]).start()

        @pl.when(jnp.logical_not(self_copy))
        def _():
            send(step).start()

    for group in range(width // 4):
        back = jnp.concatenate(
            [stage[pl.ds((4 * group + m) * PITCH, WINLEN), :] for m in range(4)], axis=0
        ).T
        parts = swap_blocks([back[WINLEN * m : WINLEN * (m + 1)] for m in range(4)])
        for m in range(4):
            for i in range(lines):
                rows = trace_rows(i, crossline(4 * group + m), width)
                shift_ref[rows, :] = parts[m][SUB * i : SUB * (i + 1)]

    for step in range(slabs):
        pltpu.make_async_copy(mine.at[0], got.at[step], recv_sem.at[step]).wait()
    for part in range(each):
        total = got[part]
        for group in range(1, groups):
            total = total + got[group * each + part]
        total_ref[part] = total

    for step in range(slabs):
        self_copy = jnp.logical_and(target_row == row, col == step)

        @pl.when(jnp.logical_not(self_copy))
        def _():
            send(step).wait_send()


def solve_small(matrix, target):
    lower = [[None] * KW for _ in range(KW)]
    inverse = [None] * KW
    for column in range(KW):
        pivot = matrix[column][column]
        for inner in range(column):
            pivot = pivot - lower[column][inner] * lower[column][inner]
        inverse[column] = lax.rsqrt(pivot)
        for target_row in range(column + 1, KW):
            entry = matrix[target_row][column]
            for inner in range(column):
                entry = entry - lower[target_row][inner] * lower[column][inner]
            lower[target_row][column] = entry * inverse[column]
    forward = []
    for column in range(KW):
        entry = target[column]
        for inner in range(column):
            entry = entry - lower[column][inner] * forward[inner]
        forward.append(entry * inverse[column])
    backward = [None] * KW
    for column in range(KW - 1, -1, -1):
        entry = forward[column]
        for inner in range(column + 1, KW):
            entry = entry - lower[inner][column] * backward[inner]
        backward[column] = entry * inverse[column]
    return backward


def finish_kernel(width, damping, shift_ref, total_ref, shift_out, delta_ref, sem):
    copy = pltpu.make_async_copy(shift_ref, shift_out, sem)
    copy.start()
    each, share = total_ref.shape[0], total_ref.shape[1]
    total = jnp.concatenate([total_ref[part] for part in range(each)], axis=0)

    def term(number):
        return total[:, number * width : (number + 1) * width]

    matrix = [[None] * KW for _ in range(KW)]
    for number, (k, j) in enumerate(PAIRS):
        matrix[k][j] = term(KW + number) + (damping if k == j else 0.0)
    delta = solve_small(matrix, [term(k) for k in range(KW)])
    for k in range(KW):
        for part in range(each):
            delta_ref[k, :, pl.ds(part * width, width)] = delta[k][part * share : (part + 1) * share]
    copy.wait()


def as_rows(block):
    lines, width, samples = block.shape
    tiles = block.reshape(lines, width // SUB, SUB, samples // LANES, LANES)
    return tiles.transpose(0, 1, 3, 2, 4).reshape(-1, LANES)


def from_rows(flat, lines, width, samples):
    tiles = flat.reshape(lines, width // SUB, samples // LANES, SUB, LANES)
    return tiles.transpose(0, 1, 3, 2, 4).reshape(lines, width, samples)


def per_device(baseline, monitor, shift_model, knot_start, half_width):
    lines, width, samples = baseline.shape
    windows = samples // WINLEN
    groups, slabs = lax.axis_size("inl"), lax.axis_size("xl")
    share, each = windows // slabs, slabs // groups
    packed = -(-(TERMS * width) // LANES) * LANES
    f32 = jnp.float32
    whole = pl.BlockSpec(memory_space=pltpu.VMEM)
    anywhere = pl.BlockSpec(memory_space=pltpu.HBM)
    base_rows, moni_rows = as_rows(baseline), as_rows(monitor)
    coef, knots = shift_model.transpose(0, 2, 1), knot_start.T
    base_rows, moni_rows, coef, knots = (
        pltpu.with_memory_space_constraint(value, pltpu.HBM) for value in (base_rows, moni_rows, coef, knots)
    )
    edges = (2, 2, HMAX * lines * SUB, LANES)
    dma = pltpu.SemaphoreType.DMA
    timed, table, model = pl.pallas_call(
        functools.partial(sums_kernel, width, lines),
        out_shape=(
            jax.ShapeDtypeStruct((WINLEN * STEP, LANES), f32),
            jax.ShapeDtypeStruct((WINLEN * LINE, LANES), f32),
            jax.ShapeDtypeStruct((KW, width, LANES), f32),
        ),
        in_specs=[anywhere] * 4,
        out_specs=(whole,) * 3,
        scratch_shapes=[
            pltpu.VMEM(base_rows.shape, f32),
            pltpu.VMEM(moni_rows.shape, f32),
            pltpu.VMEM(coef.shape, f32),
            pltpu.VMEM(knots.shape, jnp.int32),
            pltpu.VMEM(edges, f32),
            pltpu.VMEM(edges, f32),
            pltpu.VMEM((2, width * PITCH, LANES), f32),
            pltpu.VMEM((BASE_ROWS + MONI_ROWS, 3 * SUB, LANES), f32),
            pltpu.VMEM((width, LANES), f32),
            dma((4,)),
            dma((2, 2)),
            dma((2, 2)),
        ],
        compiler_params=pltpu.CompilerParams(
            collective_id=1, has_side_effects=True, vmem_limit_bytes=12 * 1024 * 1024
        ),
        name="sums",
    )(base_rows, moni_rows, coef, knots)
    shift, total = pl.pallas_call(
        functools.partial(lags_kernel, groups, slabs, width, lines),
        out_shape=(
            jax.ShapeDtypeStruct(base_rows.shape, f32),
            jax.ShapeDtypeStruct((each, share, packed), f32),
        ),
        in_specs=[pl.BlockSpec(memory_space=pltpu.SMEM)] + [whole] * 3,
        out_specs=(whole, whole),
        scratch_shapes=[
            pltpu.VMEM((width * PITCH, LANES), f32),
            pltpu.VMEM((WINLEN + 2 * LAGS, width, LANES), f32),
            pltpu.VMEM((TERMS, width, LANES), f32),
            pltpu.VMEM((packed, LANES), f32),
            pltpu.VMEM((slabs, share, packed), f32),
            pltpu.VMEM((slabs, share, packed), f32),
            dma((slabs,)),
            dma((slabs,)),
        ],
        compiler_params=pltpu.CompilerParams(
            collective_id=0, has_side_effects=True, vmem_limit_bytes=12 * 1024 * 1024
        ),
        name="lags",
    )(half_width, timed, table, model)
    shift, delta = pl.pallas_call(
        functools.partial(finish_kernel, width, DAMPING * lines * groups),
        out_shape=(
            jax.ShapeDtypeStruct(base_rows.shape, f32),
            jax.ShapeDtypeStruct((KW, share, each * width), f32),
        ),
        in_specs=[whole, whole],
        out_specs=(anywhere, whole),
        scratch_shapes=[dma],
        compiler_params=pltpu.CompilerParams(vmem_limit_bytes=8 * 1024 * 1024),
        name="finish",
    )(shift, total)
    return (from_rows(shift, lines, width, samples), delta)


def solution(mesh):
    in_specs = (P("inl", "xl", None), P("inl", "xl", None), P(None, None, "xl"), P(), P("xl"))
    out_specs = (P("inl", "xl", None), P(None, "xl", "inl"))
    return jax.shard_map(
        per_device, mesh=mesh, in_specs=in_specs, out_specs=out_specs, check_vma=False
    )
```

```python
import functools
import math

import jax
import jax.numpy as jnp
from jax import lax
from jax.experimental import pallas as pl
from jax.experimental.pallas import tpu as pltpu
from jax.sharding import PartitionSpec as P

LAGS = 15
TWIN = 12
HMAX = 3
WINLEN = 32
KW = 4
KSTEP = 8
EPSILON = 1e-06
SHARPNESS = 6.0
DAMPING = 0.5

LANES = 128
SUB = 8
REACH = LAGS + TWIN
NLAG = 2 * LAGS + 1
PAIRS = [(k, j) for k in range(KW) for j in range(k + 1)]
TERMS = KW + len(PAIRS)
MESH_ID = pl.DeviceIdType.MESH

TILES = 7
BLOCK = TILES * SUB
EVEN, ODD, ZERO, BOTH = SUB, 3 * SUB, 5 * SUB, 6 * SUB
ENERGY = 3
SLOTS = ENERGY + NLAG
STEP = SLOTS * BLOCK + SUB
BASE_ROWS = WINLEN + 2 * TWIN
MONI_ROWS = WINLEN + 2 * REACH
HALO = [(1, 0), (1, 2), None, (0, 1), (1, 1), None, (0, 0), (0, 2)]
PITCH = WINLEN + 1
LINE = 2 * SUB + 1
SCALE = SHARPNESS * math.log2(math.e)


def spline(offset):
    square = offset * offset
    cubed = square * offset
    piece_one = cubed / 6.0
    piece_two = (-3.0 * cubed + 12.0 * square - 12.0 * offset + 4.0) / 6.0
    piece_three = (3.0 * cubed - 24.0 * square + 60.0 * offset - 44.0) / 6.0
    remain = 4.0 - offset
    piece_four = remain * remain * remain / 6.0
    result = jnp.where(offset < 4.0, piece_four, 0.0 * offset)
    result = jnp.where(offset < 3.0, piece_three, result)
    result = jnp.where(offset < 2.0, piece_two, result)
    result = jnp.where(offset < 1.0, piece_one, result)
    return jnp.where(offset < 0.0, 0.0 * offset, result)


def plus(left, right):
    return tuple(x + y for x, y in zip(left, right))


def box_sums(term, put):
    outs = WINLEN // SUB
    terms, totals, suffixes = {}, {}, {}

    def block(number):
        if number not in terms:
            terms[number] = [term(number * SUB + j) for j in range(SUB)]
        return terms[number]

    def suffix(number):
        if number not in suffixes:
            vals = list(block(number))
            for j in range(SUB - 2, -1, -1):
                vals[j] = plus(vals[j], vals[j + 1])
            suffixes[number] = vals
            totals[number] = vals[0]
        return suffixes[number]

    def total(number):
        if number not in totals:
            vals = block(number)
            while len(vals) > 1:
                vals = [plus(vals[2 * j], vals[2 * j + 1]) for j in range(len(vals) // 2)]
            totals[number] = vals[0]
        return totals[number]

    for number in range(outs):
        tail = suffix(number)
        for later in (number + 1, number + 2):
            if later < outs:
                suffix(later)
        run = plus(total(number + 1), total(number + 2))
        for j in range(SUB):
            value = block(number + 3)[j] if number + 3 < outs + 2 else term((number + 3) * SUB + j)
            run = plus(run, value)
            put(number * SUB + j, plus(tail[j], run))


def trace_rows(i, x, width):
    return pl.ds((i * (width // SUB) + x // SUB) * SUB * SUB + x % SUB, SUB, stride=SUB)


def edge_tile(j, i, lines):
    return pl.ds((j * lines + i) * SUB, SUB)


def swap_blocks(parts):
    block = lax.broadcasted_iota(jnp.int32, parts[0].shape, 1) // WINLEN
    low, even = block < 2, block % 2 == 0
    w, x, y, z = parts
    w, y = jnp.where(low, w, pltpu.roll(y, 64, 1)), jnp.where(low, pltpu.roll(w, 64, 1), y)
    x, z = jnp.where(low, x, pltpu.roll(z, 64, 1)), jnp.where(low, pltpu.roll(x, 64, 1), z)
    w, x = jnp.where(even, w, pltpu.roll(x, 32, 1)), jnp.where(even, pltpu.roll(w, 96, 1), x)
    y, z = jnp.where(even, y, pltpu.roll(z, 32, 1)), jnp.where(even, pltpu.roll(y, 96, 1), z)
    return [w, x, y, z]


def crossline(slot):
    return 2 * slot if slot < SUB else 2 * (slot - SUB) + 1


def sums_kernel(
    width, lines,
    base_hbm, moni_hbm, coef_hbm, knot_hbm, timed, table, model,
    base_in, moni_in, coef_in, knot_in, edge, held, stage, wide, natural,
    in_sem, halo_send, halo_recv,
):
    row, col = lax.axis_index("inl"), lax.axis_index("xl")
    last = lax.axis_size("xl") - 1
    has_left, has_right = col > 0, col < last
    barrier = pltpu.get_barrier_semaphore()
    zeros = jnp.zeros((SUB, LANES), jnp.float32)

    loads = [
        pltpu.make_async_copy(src, dst, in_sem.at[number])
        for number, (src, dst) in enumerate(
            ((base_hbm, base_in), (moni_hbm, moni_in), (coef_hbm, coef_in), (knot_hbm, knot_in))
        )
    ]
    @pl.when(has_left)
    def _():
        pl.semaphore_signal(barrier, inc=1, device_id=(row, col - 1), device_id_type=MESH_ID)

    @pl.when(has_right)
    def _():
        pl.semaphore_signal(barrier, inc=1, device_id=(row, col + 1), device_id_type=MESH_ID)

    for load in loads:
        load.start()

    @pl.when(jnp.logical_not(has_left))
    def _():
        held[0] = jnp.zeros(held.shape[1:], jnp.float32)

    @pl.when(jnp.logical_not(has_right))
    def _():
        held[1] = jnp.zeros(held.shape[1:], jnp.float32)

    @pl.loop(0, SLOTS)
    def _(slot):
        for u in range(WINLEN):
            timed[pl.ds(u * STEP + slot * BLOCK + ZERO, SUB), :] = zeros

    loads[0].wait()
    loads[1].wait()

    for side, first in ((0, width - HMAX), (1, 0)):
        for which, ref in enumerate((base_in, moni_in)):
            for j in range(HMAX):
                for i in range(lines):
                    edge[side, which, edge_tile(j, i, lines), :] = ref[trace_rows(i, first + j, width), :]

    pl.semaphore_wait(barrier, (col + last) // (last + 1) + (last - col + last) // (last + 1))

    def halo_copy(side, which):
        return pltpu.make_async_remote_copy(
            src_ref=edge.at[side, which],
            dst_ref=held.at[side, which],
            send_sem=halo_send.at[side, which],
            recv_sem=halo_recv.at[side, which],
            device_id=(row, col + 1 if side == 0 else col - 1),
            device_id_type=MESH_ID,
        )

    def halo_wait(which):
        for side, here in ((0, has_left), (1, has_right)):

            @pl.when(here)
            def _(side=side):
                pltpu.make_async_copy(edge.at[side, which], held.at[side, which], halo_recv.at[side, which]).wait()

    for which in (1, 0):
        for side, there in ((0, has_right), (1, has_left)):

            @pl.when(there)
            def _(side=side, which=which):
                halo_copy(side, which).start()

    lane = lax.broadcasted_iota(jnp.int32, (SUB, LANES), 1)
    block, tile = lane // WINLEN, lane % SUB
    not_first, not_last = block > 0, block < 3
    has_before, has_after = (tile > 0).astype(jnp.float32), (tile < SUB - 1).astype(jnp.float32)
    inputs = ((base_in, 0, TWIN), (moni_in, BASE_ROWS, REACH))

    def spread_parts(fetch, start, part_count, first_part):
        for which, (ref, origin, halo) in ((1, inputs[1]), (0, inputs[0])):
            if first_part:
                halo_wait(which)
            for group in range(2 * part_count):
                parts = [
                    jnp.concatenate([fetch(which, ref, i, start + 4 * group + m) for i in range(lines)], axis=0)
                    for m in range(4)
                ]
                turned = jnp.concatenate(swap_blocks(parts), axis=0).T
                for m in range(4):
                    stage[which, pl.ds((4 * group + m) * PITCH, WINLEN), :] = turned[m * WINLEN : (m + 1) * WINLEN]
            for u in range(WINLEN):
                for part in range(part_count):
                    band = pl.ds((first_part + part) * SUB, SUB)
                    value = stage[which, pl.ds(part * SUB * PITCH + u, SUB, stride=PITCH), :]
                    wide[origin + halo + u, band, :] = value
                    if u >= WINLEN - halo:
                        wide[origin + halo + u - WINLEN, band, :] = jnp.where(
                            not_first, pltpu.roll(value, 32, 1), pltpu.roll(value, 33, 1) * has_before
                        )
                    if u < halo:
                        wide[origin + halo + u + WINLEN, band, :] = jnp.where(
                            not_last, pltpu.roll(value, 96, 1), pltpu.roll(value, 95, 1) * has_after
                        )

    spread_parts(lambda which, ref, i, slot: ref[trace_rows(i, crossline(slot), width), :], 0, 2, 0)

    loads[2].wait()
    loads[3].wait()
    sample = lax.broadcasted_iota(jnp.int32, (WINLEN, LANES), 0).astype(jnp.float32)
    windows = knot_in.shape[1]
    window = lax.broadcasted_iota(jnp.int32, (windows, LANES), 0)
    column = lax.broadcasted_iota(jnp.int32, (windows, LANES), 1)
    pick = (window == 4 * (column % SUB) + column // WINLEN).astype(jnp.float32)

    def spread(values):
        return lax.dot_general(
            values, pick, (((1,), (0,)), ((), ())),
            precision=lax.Precision.HIGHEST, preferred_element_type=jnp.float32,
        )

    starts = spread(knot_in[...].astype(jnp.float32))
    phi = [spline((sample - starts[k : k + 1]) / KSTEP) for k in range(KW)]
    for k in range(KW):
        table[pl.ds(k, WINLEN, stride=LINE), :] = phi[k]
        natural[...] = spread(coef_in[k])
        for part in range(2):
            model[k, pl.ds(part * SUB, SUB), :] = natural[pl.ds(part, SUB, stride=2), :]
    for number, (k, j) in enumerate(PAIRS):
        table[pl.ds(KW + number, WINLEN, stride=LINE), :] = phi[k] * phi[j]

    def operands(slot):
        moni_energy = jnp.where(slot == 2, BASE_ROWS + 2 * LAGS, BASE_ROWS)
        is_moni = jnp.logical_or(slot == 1, slot == 2)
        first = jnp.where(is_moni, moni_energy, 0)
        second = jnp.where(slot == 0, 0, jnp.where(is_moni, moni_energy, BASE_ROWS + slot - ENERGY))
        return first, second

    def each_slot(tile, keep):
        band = pl.ds(tile * SUB, SUB)

        def single(slot):
            first, second = operands(slot)

            def term(r):
                return (wide[first + r, band, :] * wide[second + r, band, :],)

            def put(u, values):
                keep(u, slot, values[0])

            box_sums(term, put)

        def double(slot):
            moni = BASE_ROWS + slot - ENERGY
            rows = {}

            def row(r):
                if r not in rows:
                    rows[r] = wide[moni + r, band, :]
                return rows[r]

            def term(r):
                value = wide[r, band, :]
                return (value * row(r), value * row(r + 1))

            def put(u, values):
                keep(u, slot, values[0])
                keep(u, slot + 1, values[1])

            box_sums(term, put)

        return single, double

    def own_keep(offset):
        def keep(u, slot, value):
            place = u * STEP + slot * BLOCK
            timed[pl.ds(place + offset, SUB), :] = value
            if offset == ODD:
                timed[pl.ds(place + BOTH, SUB), :] = timed[pl.ds(place + EVEN, SUB), :] + value

        return keep

    own = [each_slot(0, own_keep(EVEN)), each_slot(1, own_keep(ODD))]

    @pl.loop(0, ENERGY + 1)
    def _(number):
        for single, _ in own:
            single(jnp.where(number < ENERGY, number, SLOTS - 1))

    @pl.loop(0, LAGS)
    def _(number):
        for _, double in own:
            double(ENERGY + 2 * number)

    def halo_trace(which, ref, i, slot):
        if HALO[slot] is None:
            return zeros
        side, j = HALO[slot]
        return held[side, which, edge_tile(j, i, lines), :]

    spread_parts(halo_trace, 0, 1, 2)

    def halo_keep(u, slot, value):
        place = u * STEP + slot * BLOCK
        timed[pl.ds(place + 4, 4), :] = value[0:4]
        timed[pl.ds(place + 2 * SUB, SUB), :] = value
        timed[pl.ds(place + 4 * SUB, 4), :] = value[4:8]

    single, double = each_slot(2, halo_keep)

    @pl.loop(0, ENERGY + 1, unroll=2)
    def _(number):
        single(jnp.where(number < ENERGY, number, SLOTS - 1))

    @pl.loop(0, LAGS)
    def _(number):
        double(ENERGY + 2 * number)

    for which in (1, 0):
        for side, there in ((0, has_right), (1, has_left)):

            @pl.when(there)
            def _(side=side, which=which):
                halo_copy(side, which).wait_send()


def lags_kernel(
    groups, slabs, width, lines,
    half_ref, timed, table, model, shift_ref, total_ref,
    stage, emoni, acc, flat, mine, got, send_sem, recv_sem,
):
    row, col = lax.axis_index("inl"), lax.axis_index("xl")
    each = slabs // groups
    target_row = col // each
    place = row * each + col % each
    barrier = pltpu.get_barrier_semaphore()
    for step in range(slabs):
        source_row, source_col = step // each, row * each + step % each

        @pl.when(jnp.logical_or(source_row != row, source_col != col))
        def _():
            pl.semaphore_signal(
                barrier, inc=1, device_id=(source_row, source_col), device_id_type=MESH_ID
            )

    half = half_ref[0]
    two, three = half >= 2, half >= 3
    near_odd = jnp.where(two, ODD - 1, ZERO)
    near_even = jnp.where(two, EVEN + 1, ZERO)
    far_even = jnp.where(three, EVEN - 1, ZERO)
    far_odd = jnp.where(three, ODD + 1, ZERO)
    end_even = jnp.where(three, ODD - 2, jnp.where(two, EVEN - 1, ODD - 1))
    end_odd = jnp.where(three, EVEN + 2, jnp.where(two, ODD + 1, EVEN + 1))

    def lateral(u, slot):
        def at(offset):
            return timed[pl.ds(u * STEP + slot * BLOCK + offset, SUB), :]

        middle = at(BOTH) + (at(near_odd) + at(near_even)) + (at(far_even) + at(far_odd))
        return middle + at(end_even), middle + at(end_odd)

    @pl.loop(0, WINLEN, unroll=4)
    def _(u):
        for slot, shift in ((1, 0), (2, 2 * LAGS)):
            for part, value in enumerate(lateral(u, slot)):
                emoni[shift + u, pl.ds(part * SUB, SUB), :] = value

    acc[...] = jnp.zeros_like(acc)
    order = list(range(LAGS)) + list(range(2 * LAGS, LAGS, -1)) + [LAGS]

    @pl.loop(0, WINLEN, unroll=4)
    def _(u):
        energy_base = [value * (1.0 / (SCALE * SCALE)) for value in lateral(u, 0)]
        run = [None, None]
        below = [None, None]
        moment = [None, None]
        corr = [None, None]
        for lag in order:
            sums = lateral(u, ENERGY + lag)
            for part in range(2):
                energy = energy_base[part] * emoni[u + lag, pl.ds(part * SUB, SUB), :]
                argument = sums[part] * lax.rsqrt(energy + EPSILON / (SCALE * SCALE))
                weight = jnp.exp2(argument)
                if lag == 2 * LAGS:
                    below[part], run[part] = run[part], None
                run[part] = weight if run[part] is None else run[part] + weight
                if lag != LAGS:
                    if moment[part] is None:
                        moment[part] = -run[part]
                    elif lag < LAGS:
                        moment[part] = moment[part] - run[part]
                    else:
                        moment[part] = moment[part] + run[part]
                product = argument * weight
                corr[part] = product if corr[part] is None else corr[part] + product
        for part in range(2):
            inverse = 1.0 / (below[part] + run[part])
            observed = moment[part] * inverse
            stage[pl.ds(part * SUB * PITCH + u, SUB, stride=PITCH), :] = observed
            conf = 0.5 + (0.5 / SCALE) * (corr[part] * inverse)
            band = pl.ds(part * SUB, SUB)
            basis = [table[pl.ds(u * LINE + k, 1), :] for k in range(TERMS)]
            tau = model[0, band, :] * basis[0]
            for k in range(1, KW):
                tau = tau + model[k, band, :] * basis[k]
            weighted = conf * (observed - tau)
            for k in range(TERMS):
                acc[k, band, :] += (weighted if k < KW else conf) * basis[k]

    for part in range(2):
        for k in range(TERMS):
            value = acc[k, pl.ds(part * SUB, SUB), :]
            value = value + pltpu.roll(value, LANES - SUB, 1)
            value = value + pltpu.roll(value, LANES - 2 * SUB, 1)
            flat[pl.ds(k * width + part, SUB, stride=2), :] = value
    spare = flat.shape[0] - TERMS * width
    if spare:
        flat[pl.ds(TERMS * width, spare), :] = jnp.zeros((spare, LANES), jnp.float32)
    turned = flat[...].T
    share = mine.shape[1]
    for owner in range(slabs):
        for j in range(share):
            number = owner * share + j
            lane_of = (number % 4) * WINLEN + number // 4
            mine[owner, j : j + 1] = turned[lane_of : lane_of + 1]

    def send(step):
        return pltpu.make_async_remote_copy(
            src_ref=mine.at[step],
            dst_ref=got.at[place],
            send_sem=send_sem.at[step],
            recv_sem=recv_sem.at[place],
            device_id=(target_row, step),
            device_id_type=MESH_ID,
        )

    away = (row - target_row) * (row - target_row)
    pl.semaphore_wait(barrier, slabs - 1 + (away + groups * groups - 1) // (groups * groups))
    for step in range(slabs):
        self_copy = jnp.logical_and(target_row == row, col == step)

        @pl.when(self_copy)
        def _():
            pltpu.make_async_copy(mine.at[col], got.at[place], recv_sem.at[place]).start()

        @pl.when(jnp.logical_not(self_copy))
        def _():
            send(step).start()

    for group in range(width // 4):
        back = jnp.concatenate(
            [stage[pl.ds((4 * group + m) * PITCH, WINLEN), :] for m in range(4)], axis=0
        ).T
        parts = swap_blocks([back[WINLEN * m : WINLEN * (m + 1)] for m in range(4)])
        for m in range(4):
            for i in range(lines):
                rows = trace_rows(i, crossline(4 * group + m), width)
                shift_ref[rows, :] = parts[m][SUB * i : SUB * (i + 1)]

    for step in range(slabs):
        pltpu.make_async_copy(mine.at[0], got.at[step], recv_sem.at[step]).wait()
    for part in range(each):
        total = got[part]
        for group in range(1, groups):
            total = total + got[group * each + part]
        total_ref[part] = total

    for step in range(slabs):
        self_copy = jnp.logical_and(target_row == row, col == step)

        @pl.when(jnp.logical_not(self_copy))
        def _():
            send(step).wait_send()


def solve_small(matrix, target):
    (p,), (q, r) = matrix[0][:1], matrix[1][:2]
    upper = 1.0 / (p * r - q * q)
    turned = [(row[0] * r - row[1] * q, row[1] * p - row[0] * q) for row in matrix[2:]]

    def reduced(row, right, whole):
        return whole - upper * (turned[row][0] * right[0] + turned[row][1] * right[1])

    s = reduced(0, matrix[2], matrix[2][2])
    t = reduced(1, matrix[2], matrix[3][2])
    v = reduced(1, matrix[3], matrix[3][3])
    first, second = (reduced(row, target, target[2 + row]) for row in range(2))
    lower = 1.0 / (s * v - t * t)
    y = lower * (v * first - t * second)
    z = lower * (s * second - t * first)
    left = target[0] - (matrix[2][0] * y + matrix[3][0] * z)
    right = target[1] - (matrix[2][1] * y + matrix[3][1] * z)
    return [upper * (r * left - q * right), upper * (p * right - q * left), y, z]


def finish_kernel(width, damping, shift_ref, total_ref, shift_out, delta_out, terms, delta_ref, sem):
    shift_copy = pltpu.make_async_copy(shift_ref, shift_out, sem.at[0])
    shift_copy.start()
    each, share = total_ref.shape[0], total_ref.shape[1]
    for number in range(TERMS):
        for part in range(each):
            terms[number, :, pl.ds(part * width, width)] = total_ref[part, :, pl.ds(number * width, width)]

    def term(number):
        return terms[number]

    matrix = [[None] * KW for _ in range(KW)]
    for number, (k, j) in enumerate(PAIRS):
        matrix[k][j] = term(KW + number) + (damping if k == j else 0.0)
    for k, value in enumerate(solve_small(matrix, [term(k) for k in range(KW)])):
        delta_ref[k] = value
    delta_copy = pltpu.make_async_copy(delta_ref, delta_out, sem.at[1])
    delta_copy.start()
    delta_copy.wait()
    shift_copy.wait()


def as_rows(block):
    lines, width, samples = block.shape
    tiles = block.reshape(lines, width // SUB, SUB, samples // LANES, LANES)
    return tiles.transpose(0, 1, 3, 2, 4).reshape(-1, LANES)


def from_rows(flat, lines, width, samples):
    tiles = flat.reshape(lines, width // SUB, samples // LANES, SUB, LANES)
    return tiles.transpose(0, 1, 3, 2, 4).reshape(lines, width, samples)


def per_device(baseline, monitor, shift_model, knot_start, half_width):
    lines, width, samples = baseline.shape
    windows = samples // WINLEN
    groups, slabs = lax.axis_size("inl"), lax.axis_size("xl")
    share, each = windows // slabs, slabs // groups
    packed = -(-(TERMS * width) // LANES) * LANES
    f32 = jnp.float32
    whole = pl.BlockSpec(memory_space=pltpu.VMEM)
    anywhere = pl.BlockSpec(memory_space=pltpu.HBM)
    base_rows, moni_rows = as_rows(baseline), as_rows(monitor)
    coef, knots = shift_model.transpose(0, 2, 1), knot_start.T
    base_rows, moni_rows, coef, knots = (
        pltpu.with_memory_space_constraint(value, pltpu.HBM) for value in (base_rows, moni_rows, coef, knots)
    )
    edges = (2, 2, HMAX * lines * SUB, LANES)
    dma = pltpu.SemaphoreType.DMA
    timed, table, model = pl.pallas_call(
        functools.partial(sums_kernel, width, lines),
        out_shape=(
            jax.ShapeDtypeStruct((WINLEN * STEP, LANES), f32),
            jax.ShapeDtypeStruct((WINLEN * LINE, LANES), f32),
            jax.ShapeDtypeStruct((KW, width, LANES), f32),
        ),
        in_specs=[anywhere] * 4,
        out_specs=(whole,) * 3,
        scratch_shapes=[
            pltpu.VMEM(base_rows.shape, f32),
            pltpu.VMEM(moni_rows.shape, f32),
            pltpu.VMEM(coef.shape, f32),
            pltpu.VMEM(knots.shape, jnp.int32),
            pltpu.VMEM(edges, f32),
            pltpu.VMEM(edges, f32),
            pltpu.VMEM((2, width * PITCH, LANES), f32),
            pltpu.VMEM((BASE_ROWS + MONI_ROWS, 3 * SUB, LANES), f32),
            pltpu.VMEM((width, LANES), f32),
            dma((4,)),
            dma((2, 2)),
            dma((2, 2)),
        ],
        compiler_params=pltpu.CompilerParams(
            collective_id=1, has_side_effects=True, vmem_limit_bytes=12 * 1024 * 1024
        ),
        name="sums",
    )(base_rows, moni_rows, coef, knots)
    shift, total = pl.pallas_call(
        functools.partial(lags_kernel, groups, slabs, width, lines),
        out_shape=(
            jax.ShapeDtypeStruct(base_rows.shape, f32),
            jax.ShapeDtypeStruct((each, share, packed), f32),
        ),
        in_specs=[pl.BlockSpec(memory_space=pltpu.SMEM)] + [whole] * 3,
        out_specs=(whole, whole),
        scratch_shapes=[
            pltpu.VMEM((width * PITCH, LANES), f32),
            pltpu.VMEM((WINLEN + 2 * LAGS, width, LANES), f32),
            pltpu.VMEM((TERMS, width, LANES), f32),
            pltpu.VMEM((packed, LANES), f32),
            pltpu.VMEM((slabs, share, packed), f32),
            pltpu.VMEM((slabs, share, packed), f32),
            dma((slabs,)),
            dma((slabs,)),
        ],
        compiler_params=pltpu.CompilerParams(
            collective_id=0, has_side_effects=True, vmem_limit_bytes=12 * 1024 * 1024
        ),
        name="lags",
    )(half_width, timed, table, model)
    shift, delta = pl.pallas_call(
        functools.partial(finish_kernel, width, DAMPING * lines * groups),
        out_shape=(
            pltpu.HBM(base_rows.shape, f32),
            pltpu.HBM((KW, share, each * width), f32),
        ),
        in_specs=[whole, whole],
        out_specs=(anywhere, anywhere),
        scratch_shapes=[
            pltpu.VMEM((TERMS, share, each * width), f32),
            pltpu.VMEM((KW, share, each * width), f32),
            dma((2,)),
        ],
        compiler_params=pltpu.CompilerParams(vmem_limit_bytes=8 * 1024 * 1024),
        name="finish",
    )(shift, total)
    return (from_rows(shift, lines, width, samples), delta)


def solution(mesh):
    in_specs = (P("inl", "xl", None), P("inl", "xl", None), P(None, None, "xl"), P(), P("xl"))
    out_specs = (P("inl", "xl", None), P(None, "xl", "inl"))
    return jax.shard_map(
        per_device, mesh=mesh, in_specs=in_specs, out_specs=out_specs, check_vma=False
    )
```

```python
import functools
import math

import jax
import jax.numpy as jnp
from jax import lax
from jax.experimental import pallas as pl
from jax.experimental.pallas import tpu as pltpu
from jax.sharding import PartitionSpec as P

LAGS = 15
TWIN = 12
HMAX = 3
WINLEN = 32
KW = 4
KSTEP = 8
EPSILON = 1e-06
SHARPNESS = 6.0
DAMPING = 0.5

LANES = 128
SUB = 8
REACH = LAGS + TWIN
NLAG = 2 * LAGS + 1
PAIRS = [(k, j) for k in range(KW) for j in range(k + 1)]
TERMS = KW + len(PAIRS)
MESH_ID = pl.DeviceIdType.MESH

TILES = 7
BLOCK = TILES * SUB
EVEN, ODD, ZERO, BOTH = SUB, 3 * SUB, 5 * SUB, 6 * SUB
ENERGY = 3
SLOTS = ENERGY + NLAG
STEP = SLOTS * BLOCK + SUB
BASE_ROWS = WINLEN + 2 * TWIN
MONI_ROWS = WINLEN + 2 * REACH
HALO = [(1, 0), (1, 2), None, (0, 1), (1, 1), None, (0, 0), (0, 2)]
PITCH = WINLEN + 1
LINE = 2 * SUB + 1
SCALE = SHARPNESS * math.log2(math.e)


def spline(offset):
    square = offset * offset
    cubed = square * offset
    piece_one = cubed / 6.0
    piece_two = (-3.0 * cubed + 12.0 * square - 12.0 * offset + 4.0) / 6.0
    piece_three = (3.0 * cubed - 24.0 * square + 60.0 * offset - 44.0) / 6.0
    remain = 4.0 - offset
    piece_four = remain * remain * remain / 6.0
    result = jnp.where(offset < 4.0, piece_four, 0.0 * offset)
    result = jnp.where(offset < 3.0, piece_three, result)
    result = jnp.where(offset < 2.0, piece_two, result)
    result = jnp.where(offset < 1.0, piece_one, result)
    return jnp.where(offset < 0.0, 0.0 * offset, result)


def plus(left, right):
    return tuple(x + y for x, y in zip(left, right))


def box_sums(term, put):
    outs = WINLEN // SUB
    terms, totals, suffixes = {}, {}, {}

    def block(number):
        if number not in terms:
            terms[number] = [term(number * SUB + j) for j in range(SUB)]
        return terms[number]

    def suffix(number):
        if number not in suffixes:
            vals = list(block(number))
            for j in range(SUB - 2, -1, -1):
                vals[j] = plus(vals[j], vals[j + 1])
            suffixes[number] = vals
            totals[number] = vals[0]
        return suffixes[number]

    def total(number):
        if number not in totals:
            vals = block(number)
            while len(vals) > 1:
                vals = [plus(vals[2 * j], vals[2 * j + 1]) for j in range(len(vals) // 2)]
            totals[number] = vals[0]
        return totals[number]

    for number in range(outs):
        tail = suffix(number)
        for later in (number + 1, number + 2):
            if later < outs:
                suffix(later)
        run = plus(total(number + 1), total(number + 2))
        for j in range(SUB):
            value = block(number + 3)[j] if number + 3 < outs + 2 else term((number + 3) * SUB + j)
            run = plus(run, value)
            put(number * SUB + j, plus(tail[j], run))


def trace_rows(i, x, width):
    return pl.ds((i * (width // SUB) + x // SUB) * SUB * SUB + x % SUB, SUB, stride=SUB)


def edge_tile(j, i, lines):
    return pl.ds((j * lines + i) * SUB, SUB)


def swap_blocks(parts):
    block = lax.broadcasted_iota(jnp.int32, parts[0].shape, 1) // WINLEN
    low, even = block < 2, block % 2 == 0
    w, x, y, z = parts
    w, y = jnp.where(low, w, pltpu.roll(y, 64, 1)), jnp.where(low, pltpu.roll(w, 64, 1), y)
    x, z = jnp.where(low, x, pltpu.roll(z, 64, 1)), jnp.where(low, pltpu.roll(x, 64, 1), z)
    w, x = jnp.where(even, w, pltpu.roll(x, 32, 1)), jnp.where(even, pltpu.roll(w, 96, 1), x)
    y, z = jnp.where(even, y, pltpu.roll(z, 32, 1)), jnp.where(even, pltpu.roll(y, 96, 1), z)
    return [w, x, y, z]


def crossline(slot):
    return 2 * slot if slot < SUB else 2 * (slot - SUB) + 1


def sums_kernel(
    width, lines,
    base_hbm, moni_hbm, coef_hbm, knot_hbm, timed, table, model,
    base_in, moni_in, coef_in, knot_in, edge, held, stage, wide, natural,
    in_sem, halo_send, halo_recv,
):
    row, col = lax.axis_index("inl"), lax.axis_index("xl")
    last = lax.axis_size("xl") - 1
    has_left, has_right = col > 0, col < last
    barrier = pltpu.get_barrier_semaphore()
    zeros = jnp.zeros((SUB, LANES), jnp.float32)

    loads = [
        pltpu.make_async_copy(src, dst, in_sem.at[number])
        for number, (src, dst) in enumerate(
            ((moni_hbm, moni_in), (base_hbm, base_in), (coef_hbm, coef_in), (knot_hbm, knot_in))
        )
    ]
    @pl.when(has_left)
    def _():
        pl.semaphore_signal(barrier, inc=1, device_id=(row, col - 1), device_id_type=MESH_ID)

    @pl.when(has_right)
    def _():
        pl.semaphore_signal(barrier, inc=1, device_id=(row, col + 1), device_id_type=MESH_ID)

    for load in loads:
        load.start()

    @pl.when(jnp.logical_not(has_left))
    def _():
        held[0] = jnp.zeros(held.shape[1:], jnp.float32)

    @pl.when(jnp.logical_not(has_right))
    def _():
        held[1] = jnp.zeros(held.shape[1:], jnp.float32)

    @pl.loop(0, SLOTS)
    def _(slot):
        for u in range(WINLEN):
            timed[pl.ds(u * STEP + slot * BLOCK + ZERO, SUB), :] = zeros

    def halo_copy(side, which):
        return pltpu.make_async_remote_copy(
            src_ref=edge.at[side, which],
            dst_ref=held.at[side, which],
            send_sem=halo_send.at[side, which],
            recv_sem=halo_recv.at[side, which],
            device_id=(row, col + 1 if side == 0 else col - 1),
            device_id_type=MESH_ID,
        )

    def halo_wait(which):
        for side, here in ((0, has_left), (1, has_right)):

            @pl.when(here)
            def _(side=side):
                pltpu.make_async_copy(edge.at[side, which], held.at[side, which], halo_recv.at[side, which]).wait()

    pl.semaphore_wait(barrier, (col + last) // (last + 1) + (last - col + last) // (last + 1))
    for which, ref, load in ((1, moni_in, loads[0]), (0, base_in, loads[1])):
        load.wait()
        for side, first, there in ((0, width - HMAX, has_right), (1, 0, has_left)):
            for j in range(HMAX):
                for i in range(lines):
                    edge[side, which, edge_tile(j, i, lines), :] = ref[trace_rows(i, first + j, width), :]

            @pl.when(there)
            def _(side=side, which=which):
                halo_copy(side, which).start()

    lane = lax.broadcasted_iota(jnp.int32, (SUB, LANES), 1)
    block, tile = lane // WINLEN, lane % SUB
    not_first, not_last = block > 0, block < 3
    has_before, has_after = (tile > 0).astype(jnp.float32), (tile < SUB - 1).astype(jnp.float32)
    inputs = ((base_in, 0, TWIN), (moni_in, BASE_ROWS, REACH))

    def spread_parts(fetch, start, part_count, first_part):
        for which, (ref, origin, halo) in ((1, inputs[1]), (0, inputs[0])):
            if first_part:
                halo_wait(which)
            for group in range(2 * part_count):
                parts = [
                    jnp.concatenate([fetch(which, ref, i, start + 4 * group + m) for i in range(lines)], axis=0)
                    for m in range(4)
                ]
                turned = jnp.concatenate(swap_blocks(parts), axis=0).T
                for m in range(4):
                    stage[which, pl.ds((4 * group + m) * PITCH, WINLEN), :] = turned[m * WINLEN : (m + 1) * WINLEN]
            for u in range(WINLEN):
                for part in range(part_count):
                    band = pl.ds((first_part + part) * SUB, SUB)
                    value = stage[which, pl.ds(part * SUB * PITCH + u, SUB, stride=PITCH), :]
                    wide[origin + halo + u, band, :] = value
                    if u >= WINLEN - halo:
                        wide[origin + halo + u - WINLEN, band, :] = jnp.where(
                            not_first, pltpu.roll(value, 32, 1), pltpu.roll(value, 33, 1) * has_before
                        )
                    if u < halo:
                        wide[origin + halo + u + WINLEN, band, :] = jnp.where(
                            not_last, pltpu.roll(value, 96, 1), pltpu.roll(value, 95, 1) * has_after
                        )

    spread_parts(lambda which, ref, i, slot: ref[trace_rows(i, crossline(slot), width), :], 0, 2, 0)

    loads[2].wait()
    loads[3].wait()
    sample = lax.broadcasted_iota(jnp.int32, (WINLEN, LANES), 0).astype(jnp.float32)
    windows = knot_in.shape[1]
    window = lax.broadcasted_iota(jnp.int32, (windows, LANES), 0)
    column = lax.broadcasted_iota(jnp.int32, (windows, LANES), 1)
    pick = (window == 4 * (column % SUB) + column // WINLEN).astype(jnp.float32)

    def spread(values):
        return lax.dot_general(
            values, pick, (((1,), (0,)), ((), ())),
            precision=lax.Precision.HIGHEST, preferred_element_type=jnp.float32,
        )

    starts = spread(knot_in[...].astype(jnp.float32))
    phi = [spline((sample - starts[k : k + 1]) / KSTEP) for k in range(KW)]
    for k in range(KW):
        table[pl.ds(k, WINLEN, stride=LINE), :] = phi[k]
        natural[...] = spread(coef_in[k])
        for part in range(2):
            model[k, pl.ds(part * SUB, SUB), :] = natural[pl.ds(part, SUB, stride=2), :]
    for number, (k, j) in enumerate(PAIRS):
        table[pl.ds(KW + number, WINLEN, stride=LINE), :] = phi[k] * phi[j]

    def operands(slot):
        moni_energy = jnp.where(slot == 2, BASE_ROWS + 2 * LAGS, BASE_ROWS)
        is_moni = jnp.logical_or(slot == 1, slot == 2)
        first = jnp.where(is_moni, moni_energy, 0)
        second = jnp.where(slot == 0, 0, jnp.where(is_moni, moni_energy, BASE_ROWS + slot - ENERGY))
        return first, second

    def each_slot(tile, keep):
        band = pl.ds(tile * SUB, SUB)

        def single(slot):
            first, second = operands(slot)

            def term(r):
                return (wide[first + r, band, :] * wide[second + r, band, :],)

            def put(u, values):
                keep(u, slot, values[0])

            box_sums(term, put)

        def double(slot):
            moni = BASE_ROWS + slot - ENERGY
            rows = {}

            def row(r):
                if r not in rows:
                    rows[r] = wide[moni + r, band, :]
                return rows[r]

            def term(r):
                value = wide[r, band, :]
                return (value * row(r), value * row(r + 1))

            def put(u, values):
                keep(u, slot, values[0])
                keep(u, slot + 1, values[1])

            box_sums(term, put)

        return single, double

    def own_keep(offset):
        def keep(u, slot, value):
            place = u * STEP + slot * BLOCK
            timed[pl.ds(place + offset, SUB), :] = value
            if offset == ODD:
                timed[pl.ds(place + BOTH, SUB), :] = timed[pl.ds(place + EVEN, SUB), :] + value

        return keep

    own = [each_slot(0, own_keep(EVEN)), each_slot(1, own_keep(ODD))]

    @pl.loop(0, ENERGY + 1)
    def _(number):
        for single, _ in own:
            single(jnp.where(number < ENERGY, number, SLOTS - 1))

    @pl.loop(0, LAGS)
    def _(number):
        for _, double in own:
            double(ENERGY + 2 * number)

    def halo_trace(which, ref, i, slot):
        if HALO[slot] is None:
            return zeros
        side, j = HALO[slot]
        return held[side, which, edge_tile(j, i, lines), :]

    spread_parts(halo_trace, 0, 1, 2)

    def halo_keep(u, slot, value):
        place = u * STEP + slot * BLOCK
        timed[pl.ds(place + 4, 4), :] = value[0:4]
        timed[pl.ds(place + 2 * SUB, SUB), :] = value
        timed[pl.ds(place + 4 * SUB, 4), :] = value[4:8]

    single, double = each_slot(2, halo_keep)

    @pl.loop(0, ENERGY + 1, unroll=2)
    def _(number):
        single(jnp.where(number < ENERGY, number, SLOTS - 1))

    @pl.loop(0, LAGS, unroll=3)
    def _(number):
        double(ENERGY + 2 * number)

    for which in (1, 0):
        for side, there in ((0, has_right), (1, has_left)):

            @pl.when(there)
            def _(side=side, which=which):
                halo_copy(side, which).wait_send()


def lags_kernel(
    groups, slabs, width, lines,
    half_ref, timed, table, model, shift_ref, total_ref,
    stage, emoni, acc, mine, got, send_sem, recv_sem,
):
    row, col = lax.axis_index("inl"), lax.axis_index("xl")
    each = slabs // groups
    target_row = col // each
    place = row * each + col % each
    barrier = pltpu.get_barrier_semaphore()
    for step in range(slabs):
        source_row, source_col = step // each, row * each + step % each

        @pl.when(jnp.logical_or(source_row != row, source_col != col))
        def _():
            pl.semaphore_signal(
                barrier, inc=1, device_id=(source_row, source_col), device_id_type=MESH_ID
            )

    half = half_ref[0]
    two, three = half >= 2, half >= 3
    near_odd = jnp.where(two, ODD - 1, ZERO)
    near_even = jnp.where(two, EVEN + 1, ZERO)
    far_even = jnp.where(three, EVEN - 1, ZERO)
    far_odd = jnp.where(three, ODD + 1, ZERO)
    end_even = jnp.where(three, ODD - 2, jnp.where(two, EVEN - 1, ODD - 1))
    end_odd = jnp.where(three, EVEN + 2, jnp.where(two, ODD + 1, EVEN + 1))

    def lateral(u, slot):
        def at(offset):
            return timed[pl.ds(u * STEP + slot * BLOCK + offset, SUB), :]

        middle = at(BOTH) + (at(near_odd) + at(near_even)) + (at(far_even) + at(far_odd))
        return middle + at(end_even), middle + at(end_odd)

    @pl.loop(0, WINLEN, unroll=8)
    def _(u):
        for slot, shift in ((1, 0), (2, 2 * LAGS)):
            for part, value in enumerate(lateral(u, slot)):
                emoni[shift + u, pl.ds(part * SUB, SUB), :] = value

    acc[...] = jnp.zeros_like(acc)
    order = list(range(LAGS)) + list(range(2 * LAGS, LAGS, -1)) + [LAGS]

    @pl.loop(0, WINLEN, unroll=4)
    def _(u):
        energy_base = [value * (1.0 / (SCALE * SCALE)) for value in lateral(u, 0)]
        run = [None, None]
        below = [None, None]
        moment = [None, None]
        corr = [None, None]
        for lag in order:
            sums = lateral(u, ENERGY + lag)
            for part in range(2):
                energy = energy_base[part] * emoni[u + lag, pl.ds(part * SUB, SUB), :]
                argument = sums[part] * lax.rsqrt(energy + EPSILON / (SCALE * SCALE))
                weight = jnp.exp2(argument)
                if lag == 2 * LAGS:
                    below[part], run[part] = run[part], None
                run[part] = weight if run[part] is None else run[part] + weight
                if lag != LAGS:
                    if moment[part] is None:
                        moment[part] = -run[part]
                    elif lag < LAGS:
                        moment[part] = moment[part] - run[part]
                    else:
                        moment[part] = moment[part] + run[part]
                product = argument * weight
                corr[part] = product if corr[part] is None else corr[part] + product
        for part in range(2):
            inverse = 1.0 / (below[part] + run[part])
            observed = moment[part] * inverse
            stage[pl.ds(part * SUB * PITCH + u, SUB, stride=PITCH), :] = observed
            conf = 0.5 + (0.5 / SCALE) * (corr[part] * inverse)
            band = pl.ds(part * SUB, SUB)
            basis = [table[pl.ds(u * LINE + k, 1), :] for k in range(TERMS)]
            tau = model[0, band, :] * basis[0]
            for k in range(1, KW):
                tau = tau + model[k, band, :] * basis[k]
            weighted = conf * (observed - tau)
            for k in range(TERMS):
                rows = pl.ds(k * width + part, SUB, stride=2)
                acc[rows, :] += (weighted if k < KW else conf) * basis[k]

    turned = acc[...].T
    share = mine.shape[1]
    for place_in in range(LANES // WINLEN):
        value = None
        for i in range(lines):
            rows = turned[place_in * WINLEN + i * SUB : place_in * WINLEN + (i + 1) * SUB]
            value = rows if value is None else value + rows
        for tile in range(SUB):
            number = tile * (LANES // WINLEN) + place_in
            mine[number // share, pl.ds(number % share, 1)] = value[tile : tile + 1]

    def send(step):
        return pltpu.make_async_remote_copy(
            src_ref=mine.at[step],
            dst_ref=got.at[place],
            send_sem=send_sem.at[step],
            recv_sem=recv_sem.at[place],
            device_id=(target_row, step),
            device_id_type=MESH_ID,
        )

    away = (row - target_row) * (row - target_row)
    pl.semaphore_wait(barrier, slabs - 1 + (away + groups * groups - 1) // (groups * groups))
    for step in range(slabs):
        self_copy = jnp.logical_and(target_row == row, col == step)

        @pl.when(self_copy)
        def _():
            pltpu.make_async_copy(mine.at[col], got.at[place], recv_sem.at[place]).start()

        @pl.when(jnp.logical_not(self_copy))
        def _():
            send(step).start()

    for group in range(width // 4):
        back = jnp.concatenate(
            [stage[pl.ds((4 * group + m) * PITCH, WINLEN), :] for m in range(4)], axis=0
        ).T
        parts = swap_blocks([back[WINLEN * m : WINLEN * (m + 1)] for m in range(4)])
        for m in range(4):
            for i in range(lines):
                rows = trace_rows(i, crossline(4 * group + m), width)
                shift_ref[rows, :] = parts[m][SUB * i : SUB * (i + 1)]

    for step in range(slabs):
        pltpu.make_async_copy(mine.at[0], got.at[step], recv_sem.at[step]).wait()
    for part in range(each):
        total = got[part]
        for group in range(1, groups):
            total = total + got[group * each + part]
        total_ref[part] = total

    for step in range(slabs):
        self_copy = jnp.logical_and(target_row == row, col == step)

        @pl.when(jnp.logical_not(self_copy))
        def _():
            send(step).wait_send()


def solve_small(matrix, target):
    (p,), (q, r) = matrix[0][:1], matrix[1][:2]
    upper = 1.0 / (p * r - q * q)
    turned = [(row[0] * r - row[1] * q, row[1] * p - row[0] * q) for row in matrix[2:]]

    def reduced(row, right, whole):
        return whole - upper * (turned[row][0] * right[0] + turned[row][1] * right[1])

    s = reduced(0, matrix[2], matrix[2][2])
    t = reduced(1, matrix[2], matrix[3][2])
    v = reduced(1, matrix[3], matrix[3][3])
    first, second = (reduced(row, target, target[2 + row]) for row in range(2))
    lower = 1.0 / (s * v - t * t)
    y = lower * (v * first - t * second)
    z = lower * (s * second - t * first)
    left = target[0] - (matrix[2][0] * y + matrix[3][0] * z)
    right = target[1] - (matrix[2][1] * y + matrix[3][1] * z)
    return [upper * (r * left - q * right), upper * (p * right - q * left), y, z]


def finish_kernel(width, damping, shift_ref, total_ref, shift_out, delta_out, terms, delta_ref, sem):
    shift_copy = pltpu.make_async_copy(shift_ref, shift_out, sem.at[0])
    shift_copy.start()
    each, share = total_ref.shape[0], total_ref.shape[1]
    for number in range(TERMS):
        for part in range(each):
            terms[number, :, pl.ds(part * width, width)] = total_ref[part, :, pl.ds(number * width, width)]

    def term(number):
        return terms[number]

    matrix = [[None] * KW for _ in range(KW)]
    for number, (k, j) in enumerate(PAIRS):
        matrix[k][j] = term(KW + number) + (damping if k == j else 0.0)
    for k, value in enumerate(solve_small(matrix, [term(k) for k in range(KW)])):
        delta_ref[k] = value
    delta_copy = pltpu.make_async_copy(delta_ref, delta_out, sem.at[1])
    delta_copy.start()
    delta_copy.wait()
    shift_copy.wait()


def as_rows(block):
    lines, width, samples = block.shape
    tiles = block.reshape(lines, width // SUB, SUB, samples // LANES, LANES)
    return tiles.transpose(0, 1, 3, 2, 4).reshape(-1, LANES)


def from_rows(flat, lines, width, samples):
    tiles = flat.reshape(lines, width // SUB, samples // LANES, SUB, LANES)
    return tiles.transpose(0, 1, 3, 2, 4).reshape(lines, width, samples)


def per_device(baseline, monitor, shift_model, knot_start, half_width):
    lines, width, samples = baseline.shape
    windows = samples // WINLEN
    groups, slabs = lax.axis_size("inl"), lax.axis_size("xl")
    share, each = windows // slabs, slabs // groups
    packed = -(-(TERMS * width) // LANES) * LANES
    f32 = jnp.float32
    whole = pl.BlockSpec(memory_space=pltpu.VMEM)
    anywhere = pl.BlockSpec(memory_space=pltpu.HBM)
    base_rows, moni_rows = as_rows(baseline), as_rows(monitor)
    coef, knots = shift_model.transpose(0, 2, 1), knot_start.T
    base_rows, moni_rows, coef, knots = (
        pltpu.with_memory_space_constraint(value, pltpu.HBM) for value in (base_rows, moni_rows, coef, knots)
    )
    edges = (2, 2, HMAX * lines * SUB, LANES)
    dma = pltpu.SemaphoreType.DMA
    timed, table, model = pl.pallas_call(
        functools.partial(sums_kernel, width, lines),
        out_shape=(
            jax.ShapeDtypeStruct((WINLEN * STEP, LANES), f32),
            jax.ShapeDtypeStruct((WINLEN * LINE, LANES), f32),
            jax.ShapeDtypeStruct((KW, width, LANES), f32),
        ),
        in_specs=[anywhere] * 4,
        out_specs=(whole,) * 3,
        scratch_shapes=[
            pltpu.VMEM(base_rows.shape, f32),
            pltpu.VMEM(moni_rows.shape, f32),
            pltpu.VMEM(coef.shape, f32),
            pltpu.VMEM(knots.shape, jnp.int32),
            pltpu.VMEM(edges, f32),
            pltpu.VMEM(edges, f32),
            pltpu.VMEM((2, width * PITCH, LANES), f32),
            pltpu.VMEM((BASE_ROWS + MONI_ROWS, 3 * SUB, LANES), f32),
            pltpu.VMEM((width, LANES), f32),
            dma((4,)),
            dma((2, 2)),
            dma((2, 2)),
        ],
        compiler_params=pltpu.CompilerParams(
            collective_id=1, has_side_effects=True, vmem_limit_bytes=12 * 1024 * 1024
        ),
        name="sums",
    )(base_rows, moni_rows, coef, knots)
    shift, total = pl.pallas_call(
        functools.partial(lags_kernel, groups, slabs, width, lines),
        out_shape=(
            jax.ShapeDtypeStruct(base_rows.shape, f32),
            jax.ShapeDtypeStruct((each, share, packed), f32),
        ),
        in_specs=[pl.BlockSpec(memory_space=pltpu.SMEM)] + [whole] * 3,
        out_specs=(whole, whole),
        scratch_shapes=[
            pltpu.VMEM((width * PITCH, LANES), f32),
            pltpu.VMEM((WINLEN + 2 * LAGS, width, LANES), f32),
            pltpu.VMEM((packed, LANES), f32),
            pltpu.VMEM((slabs, share, packed), f32),
            pltpu.VMEM((slabs, share, packed), f32),
            dma((slabs,)),
            dma((slabs,)),
        ],
        compiler_params=pltpu.CompilerParams(
            collective_id=0, has_side_effects=True, vmem_limit_bytes=12 * 1024 * 1024
        ),
        name="lags",
    )(half_width, timed, table, model)
    shift, delta = pl.pallas_call(
        functools.partial(finish_kernel, width, DAMPING * lines * groups),
        out_shape=(
            pltpu.HBM(base_rows.shape, f32),
            pltpu.HBM((KW, share, each * width), f32),
        ),
        in_specs=[whole, whole],
        out_specs=(anywhere, anywhere),
        scratch_shapes=[
            pltpu.VMEM((TERMS, share, each * width), f32),
            pltpu.VMEM((KW, share, each * width), f32),
            dma((2,)),
        ],
        compiler_params=pltpu.CompilerParams(vmem_limit_bytes=8 * 1024 * 1024),
        name="finish",
    )(shift, total)
    return (from_rows(shift, lines, width, samples), delta)


def solution(mesh):
    in_specs = (P("inl", "xl", None), P("inl", "xl", None), P(None, None, "xl"), P(), P("xl"))
    out_specs = (P("inl", "xl", None), P(None, "xl", "inl"))
    return jax.shard_map(
        per_device, mesh=mesh, in_specs=in_specs, out_specs=out_specs, check_vma=False
    )
```

```python
import functools
import math

import jax
import jax.numpy as jnp
from jax import lax
from jax.experimental import pallas as pl
from jax.experimental.pallas import tpu as pltpu
from jax.sharding import PartitionSpec as P

LAGS = 15
TWIN = 12
HMAX = 3
WINLEN = 32
KW = 4
KSTEP = 8
EPSILON = 1e-06
SHARPNESS = 6.0
DAMPING = 0.5

LANES = 128
SUB = 8
REACH = LAGS + TWIN
NLAG = 2 * LAGS + 1
PAIRS = [(k, j) for k in range(KW) for j in range(k + 1)]
TERMS = KW + len(PAIRS)
MESH_ID = pl.DeviceIdType.MESH

TILES = 7
BLOCK = TILES * SUB
EVEN, ODD, ZERO, BOTH = SUB, 3 * SUB, 5 * SUB, 6 * SUB
ENERGY = 3
SLOTS = ENERGY + NLAG
STEP = SLOTS * BLOCK + SUB
BASE_ROWS = WINLEN + 2 * TWIN
MONI_ROWS = WINLEN + 2 * REACH
HALO = [(1, 0), (1, 2), None, (0, 1), (1, 1), None, (0, 0), (0, 2)]
PITCH = WINLEN + 1
LINE = 2 * SUB + 1
SCALE = SHARPNESS * math.log2(math.e)


def spline(offset):
    square = offset * offset
    cubed = square * offset
    piece_one = cubed / 6.0
    piece_two = (-3.0 * cubed + 12.0 * square - 12.0 * offset + 4.0) / 6.0
    piece_three = (3.0 * cubed - 24.0 * square + 60.0 * offset - 44.0) / 6.0
    remain = 4.0 - offset
    piece_four = remain * remain * remain / 6.0
    result = jnp.where(offset < 4.0, piece_four, 0.0 * offset)
    result = jnp.where(offset < 3.0, piece_three, result)
    result = jnp.where(offset < 2.0, piece_two, result)
    result = jnp.where(offset < 1.0, piece_one, result)
    return jnp.where(offset < 0.0, 0.0 * offset, result)


def plus(left, right):
    return tuple(x + y for x, y in zip(left, right))


def box_sums(term, put):
    outs = WINLEN // SUB
    terms, totals, suffixes = {}, {}, {}

    def block(number):
        if number not in terms:
            terms[number] = [term(number * SUB + j) for j in range(SUB)]
        return terms[number]

    def suffix(number):
        if number not in suffixes:
            vals = list(block(number))
            for j in range(SUB - 2, -1, -1):
                vals[j] = plus(vals[j], vals[j + 1])
            suffixes[number] = vals
            totals[number] = vals[0]
        return suffixes[number]

    def total(number):
        if number not in totals:
            vals = block(number)
            while len(vals) > 1:
                vals = [plus(vals[2 * j], vals[2 * j + 1]) for j in range(len(vals) // 2)]
            totals[number] = vals[0]
        return totals[number]

    for number in range(outs):
        tail = suffix(number)
        for later in (number + 1, number + 2):
            if later < outs:
                suffix(later)
        run = plus(total(number + 1), total(number + 2))
        for j in range(SUB):
            value = block(number + 3)[j] if number + 3 < outs + 2 else term((number + 3) * SUB + j)
            run = plus(run, value)
            put(number * SUB + j, plus(tail[j], run))


def trace_rows(i, x, width):
    return pl.ds((i * (width // SUB) + x // SUB) * SUB * SUB + x % SUB, SUB, stride=SUB)


def edge_tile(j, i, lines):
    return pl.ds((j * lines + i) * SUB, SUB)


def swap_blocks(parts):
    block = lax.broadcasted_iota(jnp.int32, parts[0].shape, 1) // WINLEN
    low, even = block < 2, block % 2 == 0
    w, x, y, z = parts
    w, y = jnp.where(low, w, pltpu.roll(y, 64, 1)), jnp.where(low, pltpu.roll(w, 64, 1), y)
    x, z = jnp.where(low, x, pltpu.roll(z, 64, 1)), jnp.where(low, pltpu.roll(x, 64, 1), z)
    w, x = jnp.where(even, w, pltpu.roll(x, 32, 1)), jnp.where(even, pltpu.roll(w, 96, 1), x)
    y, z = jnp.where(even, y, pltpu.roll(z, 32, 1)), jnp.where(even, pltpu.roll(y, 96, 1), z)
    return [w, x, y, z]


def crossline(slot):
    return 2 * slot if slot < SUB else 2 * (slot - SUB) + 1


def sums_kernel(
    width, lines,
    base_hbm, moni_hbm, coef_hbm, knot_hbm, timed, table, model,
    base_in, moni_in, coef_in, knot_in, edge, held, stage, wide, natural,
    in_sem, halo_send, halo_recv,
):
    row, col = lax.axis_index("inl"), lax.axis_index("xl")
    last = lax.axis_size("xl") - 1
    has_left, has_right = col > 0, col < last
    barrier = pltpu.get_barrier_semaphore()
    zeros = jnp.zeros((SUB, LANES), jnp.float32)

    loads = [
        pltpu.make_async_copy(src, dst, in_sem.at[number])
        for number, (src, dst) in enumerate(
            ((moni_hbm, moni_in), (base_hbm, base_in), (coef_hbm, coef_in), (knot_hbm, knot_in))
        )
    ]
    @pl.when(has_left)
    def _():
        pl.semaphore_signal(barrier, inc=1, device_id=(row, col - 1), device_id_type=MESH_ID)

    @pl.when(has_right)
    def _():
        pl.semaphore_signal(barrier, inc=1, device_id=(row, col + 1), device_id_type=MESH_ID)

    for load in loads:
        load.start()

    @pl.when(jnp.logical_not(has_left))
    def _():
        held[0] = jnp.zeros(held.shape[1:], jnp.float32)

    @pl.when(jnp.logical_not(has_right))
    def _():
        held[1] = jnp.zeros(held.shape[1:], jnp.float32)

    @pl.loop(0, SLOTS)
    def _(slot):
        for u in range(WINLEN):
            timed[pl.ds(u * STEP + slot * BLOCK + ZERO, SUB), :] = zeros

    def halo_copy(side, which):
        return pltpu.make_async_remote_copy(
            src_ref=edge.at[side, which],
            dst_ref=held.at[side, which],
            send_sem=halo_send.at[side, which],
            recv_sem=halo_recv.at[side, which],
            device_id=(row, col + 1 if side == 0 else col - 1),
            device_id_type=MESH_ID,
        )

    def halo_wait(which):
        for side, here in ((0, has_left), (1, has_right)):

            @pl.when(here)
            def _(side=side):
                pltpu.make_async_copy(edge.at[side, which], held.at[side, which], halo_recv.at[side, which]).wait()

    for which, ref, load in ((1, moni_in, loads[0]), (0, base_in, loads[1])):
        load.wait()
        for side, first in ((0, width - HMAX), (1, 0)):
            for j in range(HMAX):
                for i in range(lines):
                    edge[side, which, edge_tile(j, i, lines), :] = ref[trace_rows(i, first + j, width), :]
        if which:
            pl.semaphore_wait(barrier, (col + last) // (last + 1) + (last - col + last) // (last + 1))
        for side, there in ((0, has_right), (1, has_left)):

            @pl.when(there)
            def _(side=side, which=which):
                halo_copy(side, which).start()

    lane = lax.broadcasted_iota(jnp.int32, (SUB, LANES), 1)
    block, tile = lane // WINLEN, lane % SUB
    not_first, not_last = block > 0, block < 3
    has_before, has_after = (tile > 0).astype(jnp.float32), (tile < SUB - 1).astype(jnp.float32)
    inputs = ((base_in, 0, TWIN), (moni_in, BASE_ROWS, REACH))

    def spread_parts(fetch, start, part_count, first_part):
        for which, (ref, origin, halo) in ((1, inputs[1]), (0, inputs[0])):
            if first_part:
                halo_wait(which)
            for group in range(2 * part_count):
                parts = [
                    jnp.concatenate([fetch(which, ref, i, start + 4 * group + m) for i in range(lines)], axis=0)
                    for m in range(4)
                ]
                turned = jnp.concatenate(swap_blocks(parts), axis=0).T
                for m in range(4):
                    stage[which, pl.ds((4 * group + m) * PITCH, WINLEN), :] = turned[m * WINLEN : (m + 1) * WINLEN]
            for u in range(WINLEN):
                for part in range(part_count):
                    band = pl.ds((first_part + part) * SUB, SUB)
                    value = stage[which, pl.ds(part * SUB * PITCH + u, SUB, stride=PITCH), :]
                    wide[origin + halo + u, band, :] = value
                    if u >= WINLEN - halo:
                        wide[origin + halo + u - WINLEN, band, :] = jnp.where(
                            not_first, pltpu.roll(value, 32, 1), pltpu.roll(value, 33, 1) * has_before
                        )
                    if u < halo:
                        wide[origin + halo + u + WINLEN, band, :] = jnp.where(
                            not_last, pltpu.roll(value, 96, 1), pltpu.roll(value, 95, 1) * has_after
                        )

    spread_parts(lambda which, ref, i, slot: ref[trace_rows(i, crossline(slot), width), :], 0, 2, 0)

    loads[2].wait()
    loads[3].wait()
    sample = lax.broadcasted_iota(jnp.int32, (WINLEN, LANES), 0).astype(jnp.float32)
    windows = knot_in.shape[1]
    window = lax.broadcasted_iota(jnp.int32, (windows, LANES), 0)
    column = lax.broadcasted_iota(jnp.int32, (windows, LANES), 1)
    pick = (window == 4 * (column % SUB) + column // WINLEN).astype(jnp.float32)

    def spread(values):
        return lax.dot_general(
            values, pick, (((1,), (0,)), ((), ())),
            precision=lax.Precision.HIGHEST, preferred_element_type=jnp.float32,
        )

    starts = spread(knot_in[...].astype(jnp.float32))
    phi = [spline((sample - starts[k : k + 1]) / KSTEP) for k in range(KW)]
    for k in range(KW):
        table[pl.ds(k, WINLEN, stride=LINE), :] = phi[k]
        natural[...] = spread(coef_in[k])
        for part in range(2):
            model[k, pl.ds(part * SUB, SUB), :] = natural[pl.ds(part, SUB, stride=2), :]
    for number, (k, j) in enumerate(PAIRS):
        table[pl.ds(KW + number, WINLEN, stride=LINE), :] = phi[k] * phi[j]

    def operands(slot):
        moni_energy = jnp.where(slot == 2, BASE_ROWS + 2 * LAGS, BASE_ROWS)
        is_moni = jnp.logical_or(slot == 1, slot == 2)
        first = jnp.where(is_moni, moni_energy, 0)
        second = jnp.where(slot == 0, 0, jnp.where(is_moni, moni_energy, BASE_ROWS + slot - ENERGY))
        return first, second

    def each_slot(tile, keep):
        band = pl.ds(tile * SUB, SUB)

        def single(slot):
            first, second = operands(slot)

            def term(r):
                return (wide[first + r, band, :] * wide[second + r, band, :],)

            def put(u, values):
                keep(u, slot, values[0])

            box_sums(term, put)

        def double(slot):
            moni = BASE_ROWS + slot - ENERGY
            rows = {}

            def row(r):
                if r not in rows:
                    rows[r] = wide[moni + r, band, :]
                return rows[r]

            def term(r):
                value = wide[r, band, :]
                return (value * row(r), value * row(r + 1))

            def put(u, values):
                keep(u, slot, values[0])
                keep(u, slot + 1, values[1])

            box_sums(term, put)

        return single, double

    def own_keep(offset):
        def keep(u, slot, value):
            place = u * STEP + slot * BLOCK
            timed[pl.ds(place + offset, SUB), :] = value
            if offset == ODD:
                timed[pl.ds(place + BOTH, SUB), :] = timed[pl.ds(place + EVEN, SUB), :] + value

        return keep

    own = [each_slot(0, own_keep(EVEN)), each_slot(1, own_keep(ODD))]

    @pl.loop(0, ENERGY + 1)
    def _(number):
        for single, _ in own:
            single(jnp.where(number < ENERGY, number, SLOTS - 1))

    @pl.loop(0, LAGS)
    def _(number):
        for _, double in own:
            double(ENERGY + 2 * number)

    def halo_trace(which, ref, i, slot):
        if HALO[slot] is None:
            return zeros
        side, j = HALO[slot]
        return held[side, which, edge_tile(j, i, lines), :]

    spread_parts(halo_trace, 0, 1, 2)

    def halo_keep(u, slot, value):
        place = u * STEP + slot * BLOCK
        timed[pl.ds(place + 4, 4), :] = value[0:4]
        timed[pl.ds(place + 2 * SUB, SUB), :] = value
        timed[pl.ds(place + 4 * SUB, 4), :] = value[4:8]

    single, double = each_slot(2, halo_keep)

    @pl.loop(0, ENERGY + 1, unroll=2)
    def _(number):
        single(jnp.where(number < ENERGY, number, SLOTS - 1))

    @pl.loop(0, LAGS, unroll=5)
    def _(number):
        double(ENERGY + 2 * number)

    for which in (1, 0):
        for side, there in ((0, has_right), (1, has_left)):

            @pl.when(there)
            def _(side=side, which=which):
                halo_copy(side, which).wait_send()


def lags_kernel(
    groups, slabs, width, lines,
    half_ref, timed, table, model, shift_ref, total_ref,
    stage, emoni, acc, mine, got, send_sem, recv_sem,
):
    row, col = lax.axis_index("inl"), lax.axis_index("xl")
    each = slabs // groups
    target_row = col // each
    place = row * each + col % each
    barrier = pltpu.get_barrier_semaphore()
    for step in range(slabs):
        source_row, source_col = step // each, row * each + step % each

        @pl.when(jnp.logical_or(source_row != row, source_col != col))
        def _():
            pl.semaphore_signal(
                barrier, inc=1, device_id=(source_row, source_col), device_id_type=MESH_ID
            )

    half = half_ref[0]
    two, three = half >= 2, half >= 3
    near_odd = jnp.where(two, ODD - 1, ZERO)
    near_even = jnp.where(two, EVEN + 1, ZERO)
    far_even = jnp.where(three, EVEN - 1, ZERO)
    far_odd = jnp.where(three, ODD + 1, ZERO)
    end_even = jnp.where(three, ODD - 2, jnp.where(two, EVEN - 1, ODD - 1))
    end_odd = jnp.where(three, EVEN + 2, jnp.where(two, ODD + 1, EVEN + 1))

    def lateral(u, slot):
        def at(offset):
            return timed[pl.ds(u * STEP + slot * BLOCK + offset, SUB), :]

        middle = at(BOTH) + (at(near_odd) + at(near_even)) + (at(far_even) + at(far_odd))
        return middle + at(end_even), middle + at(end_odd)

    @pl.loop(0, WINLEN, unroll=8)
    def _(u):
        for slot, shift in ((1, 0), (2, 2 * LAGS)):
            for part, value in enumerate(lateral(u, slot)):
                emoni[shift + u, pl.ds(part * SUB, SUB), :] = value

    acc[...] = jnp.zeros_like(acc)
    order = list(range(LAGS)) + list(range(2 * LAGS, LAGS, -1)) + [LAGS]

    @pl.loop(0, WINLEN, unroll=4)
    def _(u):
        energy_base = [value * (1.0 / (SCALE * SCALE)) for value in lateral(u, 0)]
        run = [None, None]
        below = [None, None]
        moment = [None, None]
        corr = [None, None]
        for lag in order:
            sums = lateral(u, ENERGY + lag)
            for part in range(2):
                energy = energy_base[part] * emoni[u + lag, pl.ds(part * SUB, SUB), :]
                argument = sums[part] * lax.rsqrt(energy + EPSILON / (SCALE * SCALE))
                weight = jnp.exp2(argument)
                if lag == 2 * LAGS:
                    below[part], run[part] = run[part], None
                run[part] = weight if run[part] is None else run[part] + weight
                if lag != LAGS:
                    if moment[part] is None:
                        moment[part] = -run[part]
                    elif lag < LAGS:
                        moment[part] = moment[part] - run[part]
                    else:
                        moment[part] = moment[part] + run[part]
                product = argument * weight
                corr[part] = product if corr[part] is None else corr[part] + product
        for part in range(2):
            inverse = 1.0 / (below[part] + run[part])
            observed = moment[part] * inverse
            stage[pl.ds(part * SUB * PITCH + u, SUB, stride=PITCH), :] = observed
            conf = 0.5 + (0.5 / SCALE) * (corr[part] * inverse)
            band = pl.ds(part * SUB, SUB)
            basis = [table[pl.ds(u * LINE + k, 1), :] for k in range(TERMS)]
            tau = model[0, band, :] * basis[0]
            for k in range(1, KW):
                tau = tau + model[k, band, :] * basis[k]
            weighted = conf * (observed - tau)
            for k in range(TERMS):
                rows = pl.ds(k * width + part, SUB, stride=2)
                acc[rows, :] += (weighted if k < KW else conf) * basis[k]

    turned = acc[...].T
    share = mine.shape[1]
    for place_in in range(LANES // WINLEN):
        value = None
        for i in range(lines):
            rows = turned[place_in * WINLEN + i * SUB : place_in * WINLEN + (i + 1) * SUB]
            value = rows if value is None else value + rows
        for tile in range(SUB):
            number = tile * (LANES // WINLEN) + place_in
            mine[number // share, pl.ds(number % share, 1)] = value[tile : tile + 1]

    def send(step):
        return pltpu.make_async_remote_copy(
            src_ref=mine.at[step],
            dst_ref=got.at[place],
            send_sem=send_sem.at[step],
            recv_sem=recv_sem.at[place],
            device_id=(target_row, step),
            device_id_type=MESH_ID,
        )

    away = (row - target_row) * (row - target_row)
    pl.semaphore_wait(barrier, slabs - 1 + (away + groups * groups - 1) // (groups * groups))
    for step in range(slabs):
        self_copy = jnp.logical_and(target_row == row, col == step)

        @pl.when(self_copy)
        def _():
            pltpu.make_async_copy(mine.at[col], got.at[place], recv_sem.at[place]).start()

        @pl.when(jnp.logical_not(self_copy))
        def _():
            send(step).start()

    for group in range(width // 4):
        back = jnp.concatenate(
            [stage[pl.ds((4 * group + m) * PITCH, WINLEN), :] for m in range(4)], axis=0
        ).T
        parts = swap_blocks([back[WINLEN * m : WINLEN * (m + 1)] for m in range(4)])
        for m in range(4):
            for i in range(lines):
                rows = trace_rows(i, crossline(4 * group + m), width)
                shift_ref[rows, :] = parts[m][SUB * i : SUB * (i + 1)]

    for step in range(slabs):
        pltpu.make_async_copy(mine.at[0], got.at[step], recv_sem.at[step]).wait()
    for part in range(each):
        total = got[part]
        for group in range(1, groups):
            total = total + got[group * each + part]
        total_ref[part] = total

    for step in range(slabs):
        self_copy = jnp.logical_and(target_row == row, col == step)

        @pl.when(jnp.logical_not(self_copy))
        def _():
            send(step).wait_send()


def solve_small(matrix, target):
    (p,), (q, r) = matrix[0][:1], matrix[1][:2]
    upper = 1.0 / (p * r - q * q)
    turned = [(row[0] * r - row[1] * q, row[1] * p - row[0] * q) for row in matrix[2:]]

    def reduced(row, right, whole):
        return whole - upper * (turned[row][0] * right[0] + turned[row][1] * right[1])

    s = reduced(0, matrix[2], matrix[2][2])
    t = reduced(1, matrix[2], matrix[3][2])
    v = reduced(1, matrix[3], matrix[3][3])
    first, second = (reduced(row, target, target[2 + row]) for row in range(2))
    lower = 1.0 / (s * v - t * t)
    y = lower * (v * first - t * second)
    z = lower * (s * second - t * first)
    left = target[0] - (matrix[2][0] * y + matrix[3][0] * z)
    right = target[1] - (matrix[2][1] * y + matrix[3][1] * z)
    return [upper * (r * left - q * right), upper * (p * right - q * left), y, z]


def finish_kernel(width, damping, shift_ref, total_ref, shift_out, delta_out, terms, delta_ref, sem):
    shift_copy = pltpu.make_async_copy(shift_ref, shift_out, sem.at[0])
    shift_copy.start()
    each, share = total_ref.shape[0], total_ref.shape[1]
    for number in range(TERMS):
        for part in range(each):
            terms[number, :, pl.ds(part * width, width)] = total_ref[part, :, pl.ds(number * width, width)]

    def term(number):
        return terms[number]

    matrix = [[None] * KW for _ in range(KW)]
    for number, (k, j) in enumerate(PAIRS):
        matrix[k][j] = term(KW + number) + (damping if k == j else 0.0)
    for k, value in enumerate(solve_small(matrix, [term(k) for k in range(KW)])):
        delta_ref[k] = value
    delta_copy = pltpu.make_async_copy(delta_ref, delta_out, sem.at[1])
    delta_copy.start()
    delta_copy.wait()
    shift_copy.wait()


def as_rows(block):
    lines, width, samples = block.shape
    tiles = block.reshape(lines, width // SUB, SUB, samples // LANES, LANES)
    return tiles.transpose(0, 1, 3, 2, 4).reshape(-1, LANES)


def from_rows(flat, lines, width, samples):
    tiles = flat.reshape(lines, width // SUB, samples // LANES, SUB, LANES)
    return tiles.transpose(0, 1, 3, 2, 4).reshape(lines, width, samples)


def per_device(baseline, monitor, shift_model, knot_start, half_width):
    lines, width, samples = baseline.shape
    windows = samples // WINLEN
    groups, slabs = lax.axis_size("inl"), lax.axis_size("xl")
    share, each = windows // slabs, slabs // groups
    packed = -(-(TERMS * width) // LANES) * LANES
    f32 = jnp.float32
    whole = pl.BlockSpec(memory_space=pltpu.VMEM)
    anywhere = pl.BlockSpec(memory_space=pltpu.HBM)
    base_rows, moni_rows = as_rows(baseline), as_rows(monitor)
    coef, knots = shift_model.transpose(0, 2, 1), knot_start.T
    base_rows, moni_rows, coef, knots = (
        pltpu.with_memory_space_constraint(value, pltpu.HBM) for value in (base_rows, moni_rows, coef, knots)
    )
    edges = (2, 2, HMAX * lines * SUB, LANES)
    dma = pltpu.SemaphoreType.DMA
    timed, table, model = pl.pallas_call(
        functools.partial(sums_kernel, width, lines),
        out_shape=(
            jax.ShapeDtypeStruct((WINLEN * STEP, LANES), f32),
            jax.ShapeDtypeStruct((WINLEN * LINE, LANES), f32),
            jax.ShapeDtypeStruct((KW, width, LANES), f32),
        ),
        in_specs=[anywhere] * 4,
        out_specs=(whole,) * 3,
        scratch_shapes=[
            pltpu.VMEM(base_rows.shape, f32),
            pltpu.VMEM(moni_rows.shape, f32),
            pltpu.VMEM(coef.shape, f32),
            pltpu.VMEM(knots.shape, jnp.int32),
            pltpu.VMEM(edges, f32),
            pltpu.VMEM(edges, f32),
            pltpu.VMEM((2, width * PITCH, LANES), f32),
            pltpu.VMEM((BASE_ROWS + MONI_ROWS, 3 * SUB, LANES), f32),
            pltpu.VMEM((width, LANES), f32),
            dma((4,)),
            dma((2, 2)),
            dma((2, 2)),
        ],
        compiler_params=pltpu.CompilerParams(
            collective_id=1, has_side_effects=True, vmem_limit_bytes=12 * 1024 * 1024
        ),
        name="sums",
    )(base_rows, moni_rows, coef, knots)
    shift, total = pl.pallas_call(
        functools.partial(lags_kernel, groups, slabs, width, lines),
        out_shape=(
            jax.ShapeDtypeStruct(base_rows.shape, f32),
            jax.ShapeDtypeStruct((each, share, packed), f32),
        ),
        in_specs=[pl.BlockSpec(memory_space=pltpu.SMEM)] + [whole] * 3,
        out_specs=(whole, whole),
        scratch_shapes=[
            pltpu.VMEM((width * PITCH, LANES), f32),
            pltpu.VMEM((WINLEN + 2 * LAGS, width, LANES), f32),
            pltpu.VMEM((packed, LANES), f32),
            pltpu.VMEM((slabs, share, packed), f32),
            pltpu.VMEM((slabs, share, packed), f32),
            dma((slabs,)),
            dma((slabs,)),
        ],
        compiler_params=pltpu.CompilerParams(
            collective_id=0, has_side_effects=True, vmem_limit_bytes=12 * 1024 * 1024
        ),
        name="lags",
    )(half_width, timed, table, model)
    shift, delta = pl.pallas_call(
        functools.partial(finish_kernel, width, DAMPING * lines * groups),
        out_shape=(
            pltpu.HBM(base_rows.shape, f32),
            pltpu.HBM((KW, share, each * width), f32),
        ),
        in_specs=[whole, whole],
        out_specs=(anywhere, anywhere),
        scratch_shapes=[
            pltpu.VMEM((TERMS, share, each * width), f32),
            pltpu.VMEM((KW, share, each * width), f32),
            dma((2,)),
        ],
        compiler_params=pltpu.CompilerParams(vmem_limit_bytes=8 * 1024 * 1024),
        name="finish",
    )(shift, total)
    return (from_rows(shift, lines, width, samples), delta)


def solution(mesh):
    in_specs = (P("inl", "xl", None), P("inl", "xl", None), P(None, None, "xl"), P(), P("xl"))
    out_specs = (P("inl", "xl", None), P(None, "xl", "inl"))
    return jax.shard_map(
        per_device, mesh=mesh, in_specs=in_specs, out_specs=out_specs, check_vma=False
    )
```
